128 devices in a mesh: seq: 8 (over x, y_hi), fsdp: 16 (over y_lo, z, core).
Axes of the slice: x: 4, y: 4 (y_hi: 2, y_lo: 2; y = y_hi * 2 + y_lo), z: 4, core: 2. Of those that a mesh axis runs over, the one named last changes fastest.
Arguments:
- patches: bfloat16 [16, 2048, 1152], P('fsdp'), may hold values from -6 to 6
- counts: int32 [16, 8], P('fsdp'), may hold values from 1 to 505, as said below
- starts: int32 [16, 8], P('fsdp'), may hold values from 0 to 1023, as said below
- embeds: bfloat16 [16, 1024, 2048], P('fsdp', 'seq'), may hold values from -6 to 6
- route_ids: int32 [16, 1024, 6], P('fsdp'), may hold values from 0 to 63, all different within a row; in each aligned block of 1024 rows (0 to 1023, 1024 to 2047, ..., all dimensions but the last counted through in order) at most 128 rows name the same one
- route_weights: float32 [16, 1024, 6], P('fsdp'), may hold values from 0.1 to 0.6
- vit_gain: float32 [1152], replicated, may hold values from 0.5 to 1.5
- vit_fc1: bfloat16 [1152, 4304], P('fsdp', 'seq'), may hold values from -0.1875 to 0.1875
- vit_fc2: bfloat16 [1152, 4304], P('fsdp', 'seq'), may hold values from -0.09375 to 0.09375
- proj_gain: float32 [4608], replicated, may hold values from 0.5 to 1.5
- proj_weight: bfloat16 [4608, 2048], P('fsdp', 'seq'), may hold values from -0.09375 to 0.09375
- moe_gain: float32 [2048], replicated, may hold values from 0.5 to 1.5
- shared_gate: bfloat16 [2048, 2816], P('fsdp', 'seq'), may hold values from -0.125 to 0.125
- shared_up: bfloat16 [2048, 2816], P('fsdp', 'seq'), may hold values from -0.125 to 0.125
- shared_down: bfloat16 [2048, 2816], P('fsdp', 'seq'), may hold values from -0.109375 to 0.109375
- expert_gate: bfloat16 [2048, 8, 1408], P('fsdp', 'seq'), may hold values from -0.125 to 0.125
- expert_up: bfloat16 [2048, 8, 1408], P('fsdp', 'seq'), may hold values from -0.125 to 0.125
- expert_down: bfloat16 [2048, 8, 1408], P('fsdp', 'seq'), may hold values from -0.15625 to 0.15625
Outputs:
- layer_out: bfloat16 [16, 1024, 2048], P('fsdp', 'seq')
The draws below stay inside these ranges and needn't reach their ends.
Inputs may be any that keep to these rules, and one draw needn't show every extreme that they name: Per stream the counts of its 8 images sum to 512. `starts`: images of a stream lie in order in disjoint runs of positions inside its 1024 positions; in each stream the 128 positions of some one index of seq are all visual. `route_ids`: the 6 experts of a token differ; in each stream no expert is chosen by more than 128 tokens.
All inputs are finite; a program needn't handle non-finite values.
Results may differ from the reference program's by a relative error of at most 0.014.
Values may be sent and summed in bfloat16 or wider, within the bound.
No kernel may reach another device: no remote copies, remote signals or barrier semaphores. Data moves between devices by JAX's collectives and lax.ppermute only.
A program may use at most 128 MiB of HBM per device.

```python
import math
import jax
import jax.numpy as jnp
import numpy as np
from jax import lax

VIT = 1152
VIT_FF = 4304
D = 2048
HID = 1408
EXPERTS = 64
TOP = 6
TOK_DEV = 128
EXP_SEQ = 1
PROJ_IN = 4608
SH_HID = 2816
WIN = 8
GROUPS = 16
SEQ_LEN = 1024
VTOK = 512
PATCHES = 2048
IMAGES = 8
ROUTE_CAP = 128
N_SEQ = 8


def image_layout(key):

    def one_stream(subkey, is_first):
        key_cut, key_owner, key_before, key_spread = jax.random.split(subkey, 4)
        random_cuts = jnp.sort(jax.random.permutation(key_cut, VTOK - 1)[:IMAGES - 1] + 1).astype(jnp.int32)
        fixed_cuts = jnp.arange(1, IMAGES, dtype=jnp.int32)
        cuts = jnp.where(is_first, fixed_cuts, random_cuts).astype(jnp.int32)
        bounds = jnp.concatenate([jnp.zeros((1,), jnp.int32), cuts, jnp.full((1,), VTOK, jnp.int32)])
        counts = (bounds[1:] - bounds[:-1]).astype(jnp.int32)
        begins = bounds[:-1]
        end_index = bounds[1:]
        owner_block = jax.random.randint(key_owner, (), 0, SEQ_LEN // TOK_DEV)
        text_slots = SEQ_LEN - VTOK
        lower_lead = jnp.maximum(0, owner_block * TOK_DEV - VTOK + TOK_DEV)
        upper_lead = jnp.minimum(text_slots, owner_block * TOK_DEV)
        before = lower_lead + jax.random.randint(key_before, (), 0, 1 << 20) % (upper_lead - lower_lead + 1)
        first_vis = owner_block * TOK_DEV - before
        spread = jnp.sort(jax.random.randint(key_spread, (IMAGES,), 0, text_slots + 1))
        covers = (end_index > first_vis) & (begins < first_vis + TOK_DEV)
        earlier = end_index <= first_vis
        text_before = jnp.where(covers, before, jnp.where(earlier, jnp.minimum(spread, before), jnp.maximum(spread, before)))
        starts = (begins + text_before).astype(jnp.int32)
        return (counts, starts)
    stream_keys = jax.random.split(jax.random.fold_in(key, 11), GROUPS)
    first_flags = jnp.arange(GROUPS, dtype=jnp.int32) == 0
    return jax.vmap(one_stream)(stream_keys, first_flags)


def draw_counts(key, part):
    return image_layout(key)[0]


def draw_starts(key, part):
    return image_layout(key)[1]


def block_levels(stream_key, extent, shards, low, high):
    factor_of = 1.0
    for dim, shards_of in shards:
        steps = jax.random.uniform(jax.random.fold_in(jax.random.fold_in(stream_key, 6), dim), (shards_of,), jnp.float32, low / len(shards), high / len(shards))
        factor_of = factor_of * jnp.repeat(jnp.exp(steps), extent[dim] // shards_of).reshape((-1,) + (1,) * (len(extent) - 1 - dim))
    return factor_of


def assign_block(stream_key, own, number, rows, number_of, top, most, lean):
    sequence = jax.random.permutation(stream_key, number_of)
    heavy_load, usual = shares(number_of, rows * top, most, lean, True), shares(number_of, rows * top, most, lean, False)
    places = jnp.arange(number_of)

    def named(sizes, offset_by):
        used = int((sizes > 0).sum())
        fixed = max(1, used // 4)
        passed = fixed + (places - fixed + offset_by * (used - fixed)) % max(1, number_of - fixed)
        return jnp.zeros((number_of,), jnp.int32).at[sequence[jnp.where(places < fixed, places, passed)]].set(jnp.asarray(sizes, jnp.int32))

    sizes = jnp.where(number % 4 == 0, named(heavy_load, number // 4), named(usual, number - number // 4 - 1))
    mixed = jax.random.permutation(jax.random.fold_in(own, 3), number_of)
    giver, sink = mixed[0:number_of // 2 * 2:2], mixed[1:number_of // 2 * 2:2]
    slack = jnp.minimum(sizes[giver] - 1, most - sizes[sink]) // 2
    slack = jnp.where((giver == sequence[0]) | (sink == sequence[0]) | (sizes[sink] == 0), 0, jnp.maximum(slack, 0))
    passed = jax.random.randint(jax.random.fold_in(own, 4), (number_of // 2,), 0, 1 << 20) % (slack + 1)
    sizes = sizes.at[giver].add(-passed).at[sink].add(passed)
    items = jnp.searchsorted(jnp.cumsum(sizes), jnp.arange(rows * top), side="right").astype(jnp.int32)
    listing = items.reshape(top, rows).T
    listing = listing[jax.random.permutation(jax.random.fold_in(own, 1), rows)]
    offset_by = jax.random.randint(jax.random.fold_in(own, 2), (rows, 1), 0, top)
    return jnp.take_along_axis(listing, (jnp.arange(top)[None, :] + offset_by) % top, axis=1)


def shares(number_of, total, reach, slope, full):
    loads = [(1 << 20) // math.isqrt(rank ** slope) + 1 for rank in range(1, number_of + 1)]
    largest = reach if full else min(reach, max(-(-total // number_of), total * loads[0] // sum(loads)))
    least = 1 if total - largest >= number_of - 1 else 0
    given, spare = [largest] + [least] * (number_of - 1), total - largest - least * (number_of - 1)
    while spare > 0:
        movable = [i for i in range(1, number_of) if given[i] < largest] or [i for i in range(1, number_of) if given[i] < reach]
        whole, budget = sum([loads[i] for i in movable]), spare
        for i in movable:
            addition = min(reach - given[i], max(1, budget * loads[i] // whole), spare)
            given[i] = given[i] + addition
            spare = spare - addition
    return np.array(given)


def scatter_about(key, extent, scale, reach, pieces=(), kind=jnp.bfloat16):
    entries = jax.random.normal(key, extent, jnp.float32) * scale
    if len(pieces) > 0:
        entries = block_levels(key, extent, pieces, -0.22, 0.18) * entries
    return jnp.clip(entries, min=-reach, max=reach).astype(kind)


def setup_inputs(seed: int = 0) -> dict:
    splits = jax.random.split(jax.random.key(seed), 19)
    patches = scatter_about(splits[0], (GROUPS, PATCHES, VIT), 1.0, 6.0, ((0, 16),))
    counts = draw_counts(jax.random.fold_in(splits[18], 71), 0)
    starts = draw_starts(jax.random.fold_in(splits[18], 71), 0)
    embeds = scatter_about(splits[3], (GROUPS, SEQ_LEN, D), 1.0, 6.0, ((0, 16), (1, 8)))
    route_ids_keys = jax.random.split(jax.random.fold_in(splits[4], 1), GROUPS * SEQ_LEN // SEQ_LEN)
    route_ids_turns = jax.random.permutation(jax.random.fold_in(splits[4], 3), GROUPS * SEQ_LEN // SEQ_LEN)
    route_ids = jax.vmap(lambda own, number: assign_block(jax.random.fold_in(splits[4], 2), own, number, SEQ_LEN, EXPERTS, TOP, ROUTE_CAP, 2))(route_ids_keys, route_ids_turns).reshape((GROUPS, SEQ_LEN, TOP))
    route_weights = jnp.clip(0.1 + 0.5 * jax.random.uniform(splits[5], (GROUPS, SEQ_LEN, TOP), jnp.float32) ** block_levels(splits[5], (GROUPS, SEQ_LEN, TOP), ((0, 16),), -0.2, 0.2), 0.1, 0.6)
    vit_gain = jnp.clip(1.0 + 0.1 * jax.random.normal(splits[6], (VIT,), jnp.float32), 0.5, 1.5)
    vit_fc1 = scatter_about(splits[7], (VIT, VIT_FF), VIT ** -0.5, 0.1875, ((0, 16), (1, 8)))
    vit_fc2 = scatter_about(splits[8], (VIT, VIT_FF), VIT_FF ** -0.5, 0.09375, ((0, 16), (1, 8)))
    proj_gain = jnp.clip(1.0 + 0.1 * jax.random.normal(splits[9], (PROJ_IN,), jnp.float32), 0.5, 1.5)
    proj_weight = scatter_about(splits[10], (PROJ_IN, D), PROJ_IN ** -0.5, 0.09375, ((0, 16), (1, 8)))
    moe_gain = jnp.clip(1.0 + 0.1 * jax.random.normal(splits[11], (D,), jnp.float32), 0.5, 1.5)
    shared_gate = scatter_about(splits[12], (D, SH_HID), D ** -0.5, 0.125, ((0, 16), (1, 8)))
    shared_up = scatter_about(splits[13], (D, SH_HID), D ** -0.5, 0.125, ((0, 16), (1, 8)))
    shared_down = scatter_about(splits[14], (D, SH_HID), SH_HID ** -0.5, 0.109375, ((0, 16), (1, 8)))
    expert_gate = scatter_about(splits[15], (D, WIN, HID), D ** -0.5, 0.125, ((0, 16), (1, 8)))
    expert_up = scatter_about(splits[16], (D, WIN, HID), D ** -0.5, 0.125, ((0, 16), (1, 8)))
    expert_down = scatter_about(splits[17], (D, WIN, HID), HID ** -0.5, 0.15625, ((0, 16), (1, 8)))
    return dict(patches=patches, counts=counts, starts=starts, embeds=embeds, route_ids=route_ids, route_weights=route_weights, vit_gain=vit_gain, vit_fc1=vit_fc1, vit_fc2=vit_fc2, proj_gain=proj_gain, proj_weight=proj_weight, moe_gain=moe_gain, shared_gate=shared_gate, shared_up=shared_up, shared_down=shared_down, expert_gate=expert_gate, expert_up=expert_up, expert_down=expert_down)


ln_epsilon = 1e-05
rms_epsilon = 1e-06

def layer_norm(values, gain_vec):
    center = values - lax.optimization_barrier(jnp.mean(values, axis=-1, keepdims=True))
    spread = lax.optimization_barrier(jnp.mean(center * center, axis=-1, keepdims=True))
    return center * lax.rsqrt(spread + ln_epsilon) * gain_vec

def rms_norm(values, gain_vec):
    square = lax.optimization_barrier(jnp.mean(values * values, axis=-1, keepdims=True))
    return values * lax.rsqrt(square + rms_epsilon) * gain_vec

def visual_positions(counts, starts, total):
    end_index = jnp.cumsum(counts).astype(jnp.int32)
    begins = (end_index - counts).astype(jnp.int32)
    token_index = jnp.arange(total, dtype=jnp.int32)
    inside = (token_index[:, None] >= begins[None, :]) & (token_index[:, None] < end_index[None, :])
    placed = starts[None, :] + token_index[:, None] - begins[None, :]
    return lax.optimization_barrier(jnp.sum(jnp.where(inside, placed, 0), axis=1)).astype(jnp.int32)

def routed_rows(gathered, route_ids, route_weights, expert, capacity, gate_w, up_w, down_w):
    hit_mask = route_ids == expert
    chosen = jnp.any(hit_mask, axis=1)
    weight_sum = lax.optimization_barrier(jnp.sum(jnp.where(hit_mask, route_weights, 0.0), axis=1))
    count_rows = gathered.shape[0]
    slot_rank = (jnp.cumsum(chosen.astype(jnp.int32)) - 1).astype(jnp.int32)
    target = jnp.where(chosen, slot_rank, capacity).astype(jnp.int32)
    slot_rows = jnp.zeros((capacity,), jnp.int32).at[target].set(jnp.arange(count_rows, dtype=jnp.int32), mode='drop')
    is_live = jnp.arange(capacity, dtype=jnp.int32) < jnp.sum(chosen.astype(jnp.int32)).astype(jnp.int32)
    picked = jnp.take(gathered, slot_rows, axis=0)
    gate_part = jnp.dot(picked, gate_w, preferred_element_type=jnp.float32)
    up_part = jnp.dot(picked, up_w, preferred_element_type=jnp.float32)
    hidden = (jax.nn.silu(gate_part) * up_part).astype(jnp.bfloat16)
    result = lax.dot_general(hidden, down_w, (((1,), (1,)), ((), ())), preferred_element_type=jnp.float32)
    factor = jnp.where(is_live, jnp.take(weight_sum, slot_rows), 0.0)
    return (slot_rows, result * factor[:, None])

def one_stream(patches, counts, starts, embeds, route_ids, route_weights, vit_gain, vit_fc1, vit_fc2, proj_gain, proj_weight, moe_gain, shared_gate, shared_up, shared_down, expert_gate, expert_up, expert_down):
    image_rows = patches.astype(jnp.float32)
    normed = layer_norm(image_rows, vit_gain).astype(jnp.bfloat16)
    hidden = jax.nn.gelu(jnp.dot(normed, vit_fc1, preferred_element_type=jnp.float32), approximate=True).astype(jnp.bfloat16)
    block_width = VIT_FF // N_SEQ
    mixed_sum = jnp.zeros(image_rows.shape, jnp.float32)
    for block_index in range(N_SEQ):
        col_start = block_index * block_width
        product = lax.dot_general(hidden[:, col_start:col_start + block_width], vit_fc2[:, col_start:col_start + block_width], (((1,), (1,)), ((), ())), preferred_element_type=jnp.float32)
        rounded = lax.optimization_barrier(product.astype(jnp.bfloat16))
        mixed_sum = mixed_sum + rounded.astype(jnp.float32)
    residual = image_rows + mixed_sum
    proj_in = layer_norm(residual.reshape(-1, PROJ_IN), proj_gain).astype(jnp.bfloat16)
    visual = jnp.dot(proj_in, proj_weight, preferred_element_type=jnp.float32).astype(jnp.bfloat16)
    positions = visual_positions(counts, starts, VTOK)
    merged = embeds.at[positions].set(visual, mode='drop')
    normed_tokens = rms_norm(merged.astype(jnp.float32), moe_gain).astype(jnp.bfloat16)
    shared_width = SH_HID // N_SEQ
    capacity = SEQ_LEN // 8
    running = jnp.zeros(merged.shape, jnp.float32)
    for block_index in range(N_SEQ):
        col_start = block_index * shared_width
        gate_part = jnp.dot(normed_tokens, shared_gate[:, col_start:col_start + shared_width], preferred_element_type=jnp.float32)
        up_part = jnp.dot(normed_tokens, shared_up[:, col_start:col_start + shared_width], preferred_element_type=jnp.float32)
        shared_hidden = (jax.nn.silu(gate_part) * up_part).astype(jnp.bfloat16)
        partial_value = lax.dot_general(shared_hidden, shared_down[:, col_start:col_start + shared_width], (((1,), (1,)), ((), ())), preferred_element_type=jnp.float32)
        for local_expert in range(EXP_SEQ):
            expert = block_index * EXP_SEQ + local_expert
            slot_rows, values = routed_rows(normed_tokens, route_ids, route_weights, expert, capacity, expert_gate[:, expert, :], expert_up[:, expert, :], expert_down[:, expert, :])
            partial_value = partial_value.at[slot_rows].add(values)
        rounded = lax.optimization_barrier(partial_value.astype(jnp.bfloat16))
        running = running + rounded.astype(jnp.float32)
    return (merged.astype(jnp.float32) + running).astype(jnp.bfloat16)

def reference(patches, counts, starts, embeds, route_ids, route_weights, vit_gain, vit_fc1, vit_fc2, proj_gain, proj_weight, moe_gain, shared_gate, shared_up, shared_down, expert_gate, expert_up, expert_down):
    streams = []
    for stream in range(GROUPS):
        streams.append(one_stream(patches[stream], counts[stream], starts[stream], embeds[stream], route_ids[stream], route_weights[stream], vit_gain, vit_fc1, vit_fc2, proj_gain, proj_weight, moe_gain, shared_gate, shared_up, shared_down, expert_gate, expert_up, expert_down))
    return jnp.stack(streams)
```

```python
import jax
import jax.numpy as jnp
from jax import lax
from jax.sharding import Mesh, PartitionSpec as P

ln_epsilon = 1e-05
rms_epsilon = 1e-06
X, YH = 4, 2
FSDP = ("yl", "z", "c")
SEQ = ("x", "yh")


def layer_norm(values, gain_vec):
    center = values - jnp.mean(values, axis=-1, keepdims=True)
    spread = jnp.mean(center * center, axis=-1, keepdims=True)
    return center * lax.rsqrt(spread + ln_epsilon) * gain_vec


def rms_norm(values, gain_vec):
    square = jnp.mean(values * values, axis=-1, keepdims=True)
    return values * lax.rsqrt(square + rms_epsilon) * gain_vec


def visual_positions(counts, starts, total):
    end_index = jnp.cumsum(counts)
    begins = end_index - counts
    token_index = jnp.arange(total, dtype=jnp.int32)
    inside = (token_index[:, None] >= begins[None, :]) & (token_index[:, None] < end_index[None, :])
    placed = starts[None, :] + token_index[:, None] - begins[None, :]
    return jnp.sum(jnp.where(inside, placed, 0), axis=1)


def shift(a, kx, ky):
    pairs = []
    for i in range(X):
        for j in range(YH):
            pairs.append((i * YH + j, ((i + kx) % X) * YH + (j + ky) % YH))
    return lax.ppermute(a, SEQ, pairs)


def dot_t(a, b):
    return lax.dot_general(a, b, (((1,), (1,)), ((), ())), preferred_element_type=jnp.float32)


def dot(a, b):
    return jnp.dot(a, b, preferred_element_type=jnp.float32)


def shards(
    patches,
    counts,
    starts,
    embeds,
    route_ids,
    route_weights,
    vit_gain,
    vit_fc1,
    vit_fc2,
    proj_gain,
    proj_weight,
    moe_gain,
    shared_gate,
    shared_up,
    shared_down,
    expert_gate,
    expert_up,
    expert_down,
):
    xi, yi = lax.axis_index("x"), lax.axis_index("yh")
    rows, width = patches.shape[1], patches.shape[2]
    half = rows // YH
    tok_dev, depth = embeds.shape[1], embeds.shape[2]
    seq_len = tok_dev * X * YH
    vtok = rows // 4
    block = vit_fc1.shape[1]

    with jax.named_scope("vit_gather"):
        vit = lax.all_gather(
            jnp.concatenate([vit_fc1, vit_fc2], axis=1), ("yh",) + FSDP, axis=0, tiled=True
        ).reshape(YH, -1, 2 * block)
    with jax.named_scope("proj_gather"):
        proj = lax.all_gather(proj_weight, ("yh",) + FSDP, axis=0, tiled=True).reshape(
            YH, -1, proj_weight.shape[1]
        )
    sh = shared_gate.shape[1]
    pad = -sh % 128
    parts = [expert_gate[:, 0], expert_up[:, 0], expert_down[:, 0]]
    parts += [jnp.pad(w, ((0, 0), (0, pad))) for w in (shared_gate, shared_up, shared_down)]
    with jax.named_scope("moe_gather"):
        moe = lax.all_gather(jnp.concatenate(parts, axis=1), FSDP, axis=0, tiled=True)
    hid = expert_gate.shape[2]
    ge, ue, de = moe[:, :hid], moe[:, hid : 2 * hid], moe[:, 2 * hid : 3 * hid]
    at = 3 * hid
    gs, us, ds = (moe[:, at + i * (sh + pad) : at + i * (sh + pad) + sh] for i in range(3))

    with jax.named_scope("embeds_gather"):
        own = embeds[0]
        pair = jnp.concatenate([own, shift(own, 0, 1)], axis=0)
        rest = [pair] + [shift(pair, k, 0) for k in range(1, X)]
        all_embeds = jnp.concatenate(rest, axis=0)

    image_rows = lax.dynamic_slice_in_dim(patches[0], yi * half, half, 0)
    normed = layer_norm(image_rows.astype(jnp.float32), vit_gain).astype(jnp.bfloat16)
    product = 0.0
    for b in range(YH):
        hidden = jax.nn.gelu(dot(normed, vit[b, :, :block]), approximate=True).astype(jnp.bfloat16)
        product = product + dot_t(hidden, vit[b, :, block:])
    sent = product.astype(jnp.bfloat16).reshape(X, half // X, width)
    got = lax.all_to_all(sent, "x", 0, 0, tiled=True)
    mixed = jnp.sum(got.astype(jnp.float32), axis=0)
    mine = lax.dynamic_slice_in_dim(patches[0], yi * half + xi * (half // X), half // X, 0)
    residual = mine.astype(jnp.float32) + mixed
    proj_in = layer_norm(residual.reshape(-1, 4 * width), proj_gain).astype(jnp.bfloat16)
    everyone = lax.all_to_all(
        jnp.broadcast_to(proj_in[None], (X,) + proj_in.shape), "x", 0, 0, tiled=True
    ).reshape(-1, 4 * width)
    visual = jnp.concatenate([dot(everyone, proj[b]) for b in range(YH)], axis=1).astype(jnp.bfloat16)
    spread = lax.all_to_all(
        jnp.broadcast_to(visual[None], (X * YH,) + visual.shape), SEQ, 0, 0, tiled=True
    )
    whole = jnp.transpose(spread.reshape(X, YH, vtok // YH, depth // X), (1, 2, 0, 3)).reshape(
        vtok, depth
    )

    where = visual_positions(counts[0], starts[0], vtok)
    blocks = []
    for kx in range(X):
        for ky in range(YH):
            owner = ((xi - kx) % X) * YH + (yi - ky) % YH
            blocks.append(owner * tok_dev + jnp.arange(tok_dev, dtype=jnp.int32))
    row_pos = jnp.concatenate(blocks)
    take = row_pos[:, None] == where[None, :]
    is_visual = jnp.any(take, axis=1)
    one_hot = take.astype(jnp.bfloat16)

    text = rms_norm(all_embeds.astype(jnp.float32), moe_gain).astype(jnp.bfloat16)
    seen = rms_norm(whole.astype(jnp.float32), moe_gain).astype(jnp.bfloat16)
    tokens = jnp.where(is_visual[:, None], dot(one_hot, seen).astype(jnp.bfloat16), text)
    merged = jnp.where(
        is_visual[:tok_dev, None], dot(one_hot[:tok_dev], whole), own.astype(jnp.float32)
    )

    expert = xi * YH + yi
    hit = route_ids[0] == expert
    chosen_abs = jnp.any(hit, axis=1)
    share_abs = jnp.sum(jnp.where(hit, route_weights[0], 0.0), axis=1)
    rank_abs = jnp.where(chosen_abs, jnp.cumsum(chosen_abs.astype(jnp.int32)) - 1, -1)

    def relative(v):
        v = v.reshape(X, YH, tok_dev)
        return jnp.concatenate(
            [
                lax.dynamic_slice(v, ((xi - kx) % X, (yi - ky) % YH, 0), (1, 1, tok_dev)).reshape(-1)
                for kx in range(X)
                for ky in range(YH)
            ]
        )

    rank, share = relative(rank_abs), relative(share_abs)
    capacity = seq_len // 8
    slots = jnp.arange(capacity, dtype=jnp.int32)
    put = rank[:, None] == slots[None, :]
    factor = jnp.sum(jnp.where(put, share[:, None], 0.0), axis=0)
    put = put.astype(jnp.bfloat16)
    picked = lax.dot_general(
        put, tokens, (((0,), (0,)), ((), ())), preferred_element_type=jnp.float32
    ).astype(jnp.bfloat16)
    expert_hidden = (jax.nn.silu(dot(picked, ge)) * dot(picked, ue)).astype(jnp.bfloat16)
    values = (dot_t(de, expert_hidden) * factor[None, :]).astype(jnp.bfloat16)
    down = jnp.concatenate([ds, values], axis=1)

    shared_hidden = (jax.nn.silu(dot(tokens, gs)) * dot(tokens, us)).astype(jnp.bfloat16)
    left = jnp.concatenate([shared_hidden, put], axis=1)
    partial = dot_t(left, down).astype(jnp.bfloat16)
    total = merged
    for kx in range(X):
        for ky in range(YH):
            at = (kx * YH + ky) * tok_dev
            piece = partial[at : at + tok_dev]
            if kx or ky:
                piece = shift(piece, -kx, -ky)
            total = total + piece.astype(jnp.float32)
    return total.astype(jnp.bfloat16)[None]


def solution(mesh):
    fine = Mesh(mesh.devices.reshape(X, YH, 2, 4, 2), SEQ + FSDP)
    placed = (
        P(FSDP, None, None),
        P(FSDP, None),
        P(FSDP, None),
        P(FSDP, SEQ, None),
        P(FSDP, None, None),
        P(FSDP, None, None),
        P(),
        P(FSDP, SEQ),
        P(FSDP, SEQ),
        P(),
        P(FSDP, SEQ),
        P(),
        P(FSDP, SEQ),
        P(FSDP, SEQ),
        P(FSDP, SEQ),
        P(FSDP, SEQ, None),
        P(FSDP, SEQ, None),
        P(FSDP, SEQ, None),
    )
    return jax.shard_map(
        shards, mesh=fine, in_specs=placed, out_specs=P(FSDP, SEQ, None), check_vma=False
    )
```

```python
import jax
import jax.numpy as jnp
from jax import lax
from jax.experimental import pallas as pl
from jax.experimental.pallas import tpu as pltpu
from jax.sharding import Mesh, PartitionSpec as P

ln_epsilon = 1e-05
rms_epsilon = 1e-06
X, YH = 4, 2
FSDP = ("yl", "z", "c")
SEQ = ("x", "yh")


def layer_norm(values, gain_vec):
    center = values - jnp.mean(values, axis=-1, keepdims=True)
    spread = jnp.mean(center * center, axis=-1, keepdims=True)
    return center * lax.rsqrt(spread + ln_epsilon) * gain_vec


def rms_norm(values, gain_vec):
    square = jnp.mean(values * values, axis=-1, keepdims=True)
    return values * lax.rsqrt(square + rms_epsilon) * gain_vec


def visual_positions(counts, starts, total):
    end_index = jnp.cumsum(counts)
    begins = end_index - counts
    token_index = jnp.arange(total, dtype=jnp.int32)
    inside = (token_index[:, None] >= begins[None, :]) & (token_index[:, None] < end_index[None, :])
    placed = starts[None, :] + token_index[:, None] - begins[None, :]
    return jnp.sum(jnp.where(inside, placed, 0), axis=1)


def shift(a, kx, ky):
    pairs = []
    for i in range(X):
        for j in range(YH):
            pairs.append((i * YH + j, ((i + kx) % X) * YH + (j + ky) % YH))
    return lax.ppermute(a, SEQ, pairs)


def dot_t(a, b):
    return lax.dot_general(a, b, (((1,), (1,)), ((), ())), preferred_element_type=jnp.float32)


def dot(a, b):
    return jnp.dot(a, b, preferred_element_type=jnp.float32)


def spread(a, axes):
    n = lax.axis_size(axes)
    return lax.all_to_all(jnp.broadcast_to(a[None], (n,) + a.shape), axes, 0, 0, tiled=True)


def tie(*arrays):
    return lax.optimization_barrier(arrays)


def ring(a, axes):
    n = lax.axis_size(axes)
    moved = [lax.ppermute(a, axes, [(i, (i + k) % n) for i in range(n)]) for k in range(1, n)]
    return [a] + moved


def swap_cores(pieces):
    return [lax.ppermute(a, "c", [(0, 1), (1, 0)]) for a in pieces]


def place_pieces(at_ref, pieces, columns, w_ref, sems):
    z_own, y_own, c_own = at_ref[0], at_ref[1], at_ref[2]
    copies = []
    for n, piece in enumerate(pieces):
        c = lax.rem(c_own + n // 4, 2)
        y = lax.rem(y_own - n % 4 + 4, 4)
        for k in range(piece.shape[0]):
            z = lax.rem(z_own - k + 4, 4)
            f = lax.rem(y, YH) * 8 + z * 2 + c
            rows = piece.shape[1]
            copies.append(
                pltpu.make_async_copy(
                    piece.at[k, :, columns],
                    w_ref.at[y // YH, pl.ds(pl.multiple_of(f * rows, rows), rows), :],
                    sems.at[n * 4 + k],
                )
            )
    for copy in copies:
        copy.start()
    return copies


def proj_kernel(at_ref, a_ref, *refs):
    pieces, (o_ref, w_ref, sems) = refs[:8], refs[8:]
    for copy in place_pieces(at_ref, pieces, slice(None), w_ref, sems):
        copy.wait()
    cols = w_ref.shape[2]
    for b in range(YH):
        o_ref[:, b * cols : (b + 1) * cols] = jnp.dot(
            a_ref[...], w_ref[b], preferred_element_type=jnp.float32
        ).astype(o_ref.dtype)


def proj_block(at, a, pieces):
    _, rows, cols = pieces[0].shape
    return pl.pallas_call(
        proj_kernel,
        grid_spec=pltpu.PrefetchScalarGridSpec(
            num_scalar_prefetch=1,
            grid=(1,),
            in_specs=[pl.BlockSpec(a.shape, lambda i, at: (0, 0))]
            + [pl.BlockSpec(memory_space=pl.ANY)] * 8,
            out_specs=pl.BlockSpec((a.shape[0], YH * cols), lambda i, at: (0, 0)),
            scratch_shapes=[
                pltpu.VMEM((YH, 16 * rows, cols), jnp.bfloat16),
                pltpu.SemaphoreType.DMA((32,)),
            ],
        ),
        out_shape=jax.ShapeDtypeStruct((a.shape[0], YH * cols), jnp.bfloat16),
        name="proj_block",
    )(at, a, *pieces)


def hidden_kernel(at_ref, n_ref, *refs):
    pieces, (o_ref, w_ref, sems) = refs[:8], refs[8:]
    sh = w_ref.shape[2] // 2
    for copy in place_pieces(at_ref, pieces, slice(0, 2 * sh), w_ref, sems):
        copy.wait()
    for b in range(YH):
        gate = jnp.dot(n_ref[...], w_ref[b, :, :sh], preferred_element_type=jnp.float32)
        up = jnp.dot(n_ref[...], w_ref[b, :, sh:], preferred_element_type=jnp.float32)
        o_ref[:, b * sh : (b + 1) * sh] = (jax.nn.silu(gate) * up).astype(o_ref.dtype)


def hidden_block(at, tokens, pieces):
    sh = pieces[0].shape[2] // 3
    return pl.pallas_call(
        hidden_kernel,
        grid_spec=pltpu.PrefetchScalarGridSpec(
            num_scalar_prefetch=1,
            grid=(1,),
            in_specs=[
                pl.BlockSpec(tokens.shape, lambda i, at: (0, 0)),
            ]
            + [pl.BlockSpec(memory_space=pl.ANY)] * 8,
            out_specs=pl.BlockSpec((tokens.shape[0], YH * sh), lambda i, at: (0, 0)),
            scratch_shapes=[
                pltpu.VMEM((YH, tokens.shape[1], 2 * sh), jnp.bfloat16),
                pltpu.SemaphoreType.DMA((32,)),
            ],
        ),
        out_shape=jax.ShapeDtypeStruct((tokens.shape[0], YH * sh), jnp.bfloat16),
        name="hidden_block",
    )(at, tokens, *pieces)


def down_kernel(at_ref, h_ref, t_ref, v_ref, u_ref, *refs):
    pieces, (o_ref, w_ref, sems) = refs[:8], refs[8:]
    sh = w_ref.shape[2]
    step = pl.program_id(0)

    @pl.when(step == 0)
    def _():
        for copy in place_pieces(at_ref, pieces, slice(2 * sh, 3 * sh), w_ref, sems):
            copy.wait()

    tok = o_ref.shape[0]
    owner = lax.rem(at_ref[3] - step + X, X) * YH + at_ref[4]
    where = owner * tok + lax.broadcasted_iota(jnp.int32, (tok, t_ref.shape[1]), 0)
    total = jnp.zeros(o_ref.shape, jnp.float32)
    for e, values in enumerate((v_ref, u_ref)):
        put = jnp.where(where == t_ref[e : e + 1, :], 1.0, 0.0).astype(jnp.bfloat16)
        total += jnp.dot(put, values[...], preferred_element_type=jnp.float32)
    for b in range(YH):
        total += lax.dot_general(
            h_ref[:, b * sh : (b + 1) * sh],
            w_ref[b],
            (((1,), (1,)), ((), ())),
            preferred_element_type=jnp.float32,
        )
    o_ref[...] = total.astype(o_ref.dtype)


def down_block(at, hidden, token_at, values, values_other, pieces):
    sh = pieces[0].shape[2] // 3
    tok, depth = hidden.shape[0] // X, values.shape[1]
    return pl.pallas_call(
        down_kernel,
        grid_spec=pltpu.PrefetchScalarGridSpec(
            num_scalar_prefetch=1,
            grid=(X,),
            in_specs=[
                pl.BlockSpec((tok, hidden.shape[1]), lambda i, at: (i, 0)),
                pl.BlockSpec(token_at.shape, lambda i, at: (0, 0)),
                pl.BlockSpec(values.shape, lambda i, at: (0, 0)),
                pl.BlockSpec(values.shape, lambda i, at: (0, 0)),
            ]
            + [pl.BlockSpec(memory_space=pl.ANY)] * 8,
            out_specs=pl.BlockSpec((tok, depth), lambda i, at: (i, 0)),
            scratch_shapes=[
                pltpu.VMEM((YH, depth, sh), jnp.bfloat16),
                pltpu.SemaphoreType.DMA((32,)),
            ],
        ),
        out_shape=jax.ShapeDtypeStruct((hidden.shape[0], depth), jnp.bfloat16),
        name="down_block",
    )(at, hidden, token_at, values, values_other, *pieces)


def vit_kernel(n_ref, w_ref, o_ref):
    wide = w_ref.shape[2] // 2
    total = jnp.zeros(o_ref.shape, jnp.float32)
    for b in range(YH):
        h = jnp.dot(n_ref[...], w_ref[b, :, :wide], preferred_element_type=jnp.float32)
        h = jax.nn.gelu(h, approximate=True).astype(jnp.bfloat16)
        total += lax.dot_general(
            h, w_ref[b, :, wide:], (((1,), (1,)), ((), ())), preferred_element_type=jnp.float32
        )
    o_ref[...] = total.astype(o_ref.dtype)


def vit_block(normed, vit):
    rows, width = normed.shape
    step = rows // X
    return pl.pallas_call(
        vit_kernel,
        grid=(X,),
        in_specs=[
            pl.BlockSpec((step, width), lambda i: (i, 0)),
            pl.BlockSpec(vit.shape, lambda i: (0, 0, 0)),
        ],
        out_specs=pl.BlockSpec((step, width), lambda i: (i, 0)),
        out_shape=jax.ShapeDtypeStruct((rows, width), jnp.bfloat16),
        name="vit_block",
    )(normed, vit)


def shards(
    patches,
    counts,
    starts,
    embeds,
    route_ids,
    route_weights,
    vit_gain,
    vit_fc1,
    vit_fc2,
    proj_gain,
    proj_weight,
    moe_gain,
    shared_gate,
    shared_up,
    shared_down,
    expert_gate,
    expert_up,
    expert_down,
):
    xi, yi = lax.axis_index("x"), lax.axis_index("yh")
    rows, width = patches.shape[1], patches.shape[2]
    half = rows // YH
    tok_dev, depth = embeds.shape[1], embeds.shape[2]
    seq_len = tok_dev * X * YH
    vtok = rows // 4
    capacity = seq_len // 8

    def padded(w):
        return jnp.pad(w, ((0, 0), (0, -w.shape[1] % 128)))

    vit_own = jnp.concatenate([padded(vit_fc1), padded(vit_fc2)], axis=1)
    wide = vit_own.shape[1] // 2
    vit = lax.all_gather(vit_own, ("yh",) + FSDP, axis=0, tiled=True).reshape(YH, -1, 2 * wide)
    experts = jnp.concatenate([expert_gate[:, 0], expert_up[:, 0], expert_down[:, 0]], axis=1)
    partner = lax.ppermute(experts, "yl", [(0, 1), (1, 0)])
    moe = lax.all_gather(
        jnp.concatenate([experts, partner], axis=1), ("z", "c"), axis=0, tiled=True
    )
    hid = expert_gate.shape[2]

    own = embeds[0]
    near = [own] + [shift(own, k, 0) for k in range(1, X)]
    other = shift(own, 0, 1)
    far = [other] + [shift(other, k, 0) for k in range(1, X)]
    proj = jnp.stack(ring(proj_weight, "z"))
    shared_own = [padded(shared_gate), padded(shared_up), padded(shared_down)]
    shared = jnp.stack(ring(jnp.concatenate(shared_own, axis=1), "z"))
    place_at = jnp.stack(
        [lax.axis_index("z"), yi * YH + lax.axis_index("yl"), lax.axis_index("c"), xi, yi]
    ).astype(jnp.int32)

    image_rows = lax.dynamic_slice_in_dim(patches[0], yi * half, half, 0)
    normed = layer_norm(image_rows.astype(jnp.float32), vit_gain).astype(jnp.bfloat16)
    vit, normed, proj, shared = tie(vit, normed, proj, shared)
    product = vit_block(normed, vit)
    product, proj, shared = tie(product, proj, shared)
    sent = product.reshape(X, half // X, width)
    got = lax.all_to_all(sent, "x", 0, 0, tiled=True)
    proj = ring(proj, ("yh", "yl"))
    shared = ring(shared, ("yh", "yl"))
    mixed = jnp.sum(got.astype(jnp.float32), axis=0)
    mine = lax.dynamic_slice_in_dim(patches[0], yi * half + xi * (half // X), half // X, 0)
    residual = mine.astype(jnp.float32) + mixed
    proj_in = layer_norm(residual.reshape(-1, 4 * width), proj_gain).astype(jnp.bfloat16)
    proj_in, proj = tie(proj_in, proj)
    everyone = spread(proj_in, "x").reshape(-1, 4 * width)
    proj = proj + swap_cores(proj)
    visual = proj_block(place_at, everyone, proj)
    visual, shared = tie(visual, shared)
    shared = shared + swap_cores(shared)
    whole = spread(visual, SEQ)
    whole = jnp.transpose(whole.reshape(X, vtok, depth // X), (1, 0, 2)).reshape(vtok, depth)

    where = visual_positions(counts[0], starts[0], vtok)

    row = jnp.arange(seq_len, dtype=jnp.int32)
    row_x = (xi - row // tok_dev % X) % X
    row_y = (yi - row // (tok_dev * X)) % YH
    row_pos = (row_x * YH + row_y) * tok_dev + row % tok_dev
    take = row_pos[:, None] == where[None, :]
    is_visual = jnp.any(take, axis=1)
    rows_here = tok_dev * X

    text = rms_norm(jnp.concatenate(near + far, axis=0).astype(jnp.float32), moe_gain)
    text = text.astype(jnp.bfloat16)
    seen = rms_norm(whole.astype(jnp.float32), moe_gain).astype(jnp.bfloat16)
    one_hot = take[:rows_here].astype(jnp.bfloat16)
    tokens = jnp.where(
        is_visual[:rows_here, None], dot(one_hot, seen).astype(jnp.bfloat16), text[:rows_here]
    )
    merged = jnp.where(
        is_visual[:tok_dev, None], dot(one_hot[:tok_dev], whole), own.astype(jnp.float32)
    )

    def ranks(expert):
        hit = route_ids[0] == expert
        chosen = jnp.any(hit, axis=1)
        share = jnp.sum(jnp.where(hit, route_weights[0], 0.0), axis=1)
        return jnp.where(chosen, jnp.cumsum(chosen.astype(jnp.int32)) - 1, -1), share

    slots = jnp.arange(capacity, dtype=jnp.int32)

    def routed(expert):
        rank, share = ranks(expert)
        place = rank[:, None] == slots[None, :]
        factor = jnp.sum(jnp.where(place, share[:, None], 0.0), axis=0)
        token_at = jnp.sum(jnp.where(place, row[:, None] + 1, 0), axis=0) - 1
        return token_at, factor

    token_at, factor = routed(xi * YH + yi)
    token_at_other, _ = routed(xi * YH + (yi + 1) % YH)
    pick_text = ((token_at[:, None] == row_pos[None, :]) & ~is_visual[None, :]).astype(jnp.bfloat16)
    pick_seen = (token_at[:, None] == where[None, :]).astype(jnp.bfloat16)
    picked = (dot(pick_text, text) + dot(pick_seen, seen)).astype(jnp.bfloat16)
    low = lax.axis_index("yl")
    side = depth // 2
    picks = [lax.dynamic_slice_in_dim(picked, l * side, side, 1) for l in (low, 1 - low)]

    def both(i):
        at = [i * hid, (i + 3) * hid]
        return dot(picks[0], moe[:, at[0] : at[0] + hid]) + dot(picks[1], moe[:, at[1] : at[1] + hid])

    expert_hidden = (jax.nn.silu(both(0)) * both(1)).astype(jnp.bfloat16)
    v_own = dot_t(expert_hidden, moe[:, 2 * hid : 3 * hid])
    v_partner = dot_t(expert_hidden, moe[:, 5 * hid : 6 * hid])
    values = jnp.concatenate(
        [jnp.where(low == 0, v_own, v_partner), jnp.where(low == 0, v_partner, v_own)], axis=1
    )
    values = (values * factor[:, None]).astype(jnp.bfloat16)
    values_other = shift(values, 0, 1)
    hidden = hidden_block(place_at, tokens, shared)
    token_ats = jnp.stack([token_at, token_at_other])
    partial = down_block(place_at, hidden, token_ats, values, values_other, shared)
    total = merged
    for kx in range(X):
        piece = partial[kx * tok_dev : (kx + 1) * tok_dev]
        if kx:
            piece = shift(piece, -kx, 0)
        total = total + piece.astype(jnp.float32)
    return total.astype(jnp.bfloat16)[None]


def solution(mesh):
    fine = Mesh(mesh.devices.reshape(X, YH, 2, 4, 2), SEQ + FSDP)
    placed = (
        P(FSDP, None, None),
        P(FSDP, None),
        P(FSDP, None),
        P(FSDP, SEQ, None),
        P(FSDP, None, None),
        P(FSDP, None, None),
        P(),
        P(FSDP, SEQ),
        P(FSDP, SEQ),
        P(),
        P(FSDP, SEQ),
        P(),
        P(FSDP, SEQ),
        P(FSDP, SEQ),
        P(FSDP, SEQ),
        P(FSDP, SEQ, None),
        P(FSDP, SEQ, None),
        P(FSDP, SEQ, None),
    )

    return jax.shard_map(
        shards, mesh=fine, in_specs=placed, out_specs=P(FSDP, SEQ, None), check_vma=False
    )
```

```python
import functools

import jax
import jax.numpy as jnp
from jax import lax
from jax.experimental import pallas as pl
from jax.experimental.pallas import tpu as pltpu
from jax.sharding import Mesh, PartitionSpec as P

ln_epsilon = 1e-05
rms_epsilon = 1e-06
X, YH = 4, 2
FSDP = ("yl", "z", "c")
SEQ = ("x", "yh")


def layer_norm(values, gain_vec):
    center = values - jnp.mean(values, axis=-1, keepdims=True)
    spread = jnp.mean(center * center, axis=-1, keepdims=True)
    return center * lax.rsqrt(spread + ln_epsilon) * gain_vec


def visual_positions(counts, starts, total):
    end_index = jnp.cumsum(counts)
    begins = end_index - counts
    token_index = jnp.arange(total, dtype=jnp.int32)
    inside = (token_index[:, None] >= begins[None, :]) & (token_index[:, None] < end_index[None, :])
    placed = starts[None, :] + token_index[:, None] - begins[None, :]
    return jnp.sum(jnp.where(inside, placed, 0), axis=1)


def shift(a, kx, ky):
    pairs = []
    for i in range(X):
        for j in range(YH):
            pairs.append((i * YH + j, ((i + kx) % X) * YH + (j + ky) % YH))
    return lax.ppermute(a, SEQ, pairs)


def dot(a, b):
    return jnp.dot(a, b, preferred_element_type=jnp.float32)


def tie(*arrays):
    return lax.optimization_barrier(arrays)


def ring(a, axes):
    n = lax.axis_size(axes)
    moved = [lax.ppermute(a, axes, [(i, (i + k) % n) for i in range(n)]) for k in range(1, n)]
    return [a] + moved


def swap_cores(pieces):
    return [lax.ppermute(a, "c", [(0, 1), (1, 0)]) for a in pieces]


def place_pieces(at_ref, pieces, columns, w_ref, sems):
    z_own, y_own, c_own = at_ref[0], at_ref[1], at_ref[2]
    copies = []
    for n, piece in enumerate(pieces):
        c = lax.rem(c_own + n // 4, 2)
        y = lax.rem(y_own - n % 4 + 4, 4)
        for k in range(piece.shape[0]):
            z = lax.rem(z_own - k + 4, 4)
            f = lax.rem(y, YH) * 8 + z * 2 + c
            rows = piece.shape[1]
            copies.append(
                pltpu.make_async_copy(
                    piece.at[k, :, columns],
                    w_ref.at[y // YH, pl.ds(pl.multiple_of(f * rows, rows), rows), :],
                    sems.at[n * 4 + k],
                )
            )
    for copy in copies:
        copy.start()
    return copies


def proj_kernel(at_ref, own_ref, left_ref, right_ref, first_ref, last_ref, *refs):
    pieces, (o_ref, a_ref, w_ref, sems) = refs[:8], refs[8:]
    copies = place_pieces(at_ref, pieces, slice(None), w_ref, sems)
    rows, some = own_ref.shape[0], first_ref.shape[0]
    for ref, back, start in (
        (own_ref, 0, 0),
        (left_ref, 1, 0),
        (right_ref, X - 1, 0),
        (first_ref, 2, 0),
        (last_ref, 2, some),
    ):
        x = lax.rem(at_ref[3] - back + X, X)
        a_ref[pl.ds(pl.multiple_of(x * rows + start, some), ref.shape[0]), :] = ref[...]
    for copy in copies:
        copy.wait()
    cols = w_ref.shape[2]
    for b in range(YH):
        o_ref[:, b * cols : (b + 1) * cols] = jnp.dot(
            a_ref[...], w_ref[b], preferred_element_type=jnp.float32
        ).astype(o_ref.dtype)


def proj_block(at, parts, pieces):
    _, rows, cols = pieces[0].shape
    count, depth = parts[0].shape
    return pl.pallas_call(
        proj_kernel,
        grid_spec=pltpu.PrefetchScalarGridSpec(
            num_scalar_prefetch=1,
            grid=(1,),
            in_specs=[pl.BlockSpec(a.shape, lambda i, at: (0, 0)) for a in parts]
            + [pl.BlockSpec(memory_space=pl.ANY)] * 8,
            out_specs=pl.BlockSpec((X * count, YH * cols), lambda i, at: (0, 0)),
            scratch_shapes=[
                pltpu.VMEM((X * count, depth), jnp.bfloat16),
                pltpu.VMEM((YH, 16 * rows, cols), jnp.bfloat16),
                pltpu.SemaphoreType.DMA((32,)),
            ],
        ),
        out_shape=jax.ShapeDtypeStruct((X * count, YH * cols), jnp.bfloat16),
        name="proj_block",
    )(at, *parts, *pieces)


def hidden_kernel(at_ref, p_ref, s_ref, t_ref, *refs):
    pieces, (o_ref, n_ref, w_ref, sems) = refs[:8], refs[8:]
    sh = w_ref.shape[2] // 2
    copies = place_pieces(at_ref, pieces, slice(0, 2 * sh), w_ref, sems)
    seen = jnp.dot(p_ref[...], s_ref[...], preferred_element_type=jnp.float32)
    n_ref[...] = seen.astype(n_ref.dtype) + t_ref[...]
    for copy in copies:
        copy.wait()
    for b in range(YH):
        gate = jnp.dot(n_ref[...], w_ref[b, :, :sh], preferred_element_type=jnp.float32)
        up = jnp.dot(n_ref[...], w_ref[b, :, sh:], preferred_element_type=jnp.float32)
        o_ref[:, b * sh : (b + 1) * sh] = (jax.nn.silu(gate) * up).astype(o_ref.dtype)


def hidden_block(at, one_hot, seen, text, pieces):
    _, rows, cols = pieces[0].shape
    sh = cols // 3
    count, depth = one_hot.shape[0], seen.shape[1]
    return pl.pallas_call(
        hidden_kernel,
        grid_spec=pltpu.PrefetchScalarGridSpec(
            num_scalar_prefetch=1,
            grid=(1,),
            in_specs=[
                pl.BlockSpec(one_hot.shape, lambda i, at: (0, 0)),
                pl.BlockSpec(seen.shape, lambda i, at: (0, 0)),
                pl.BlockSpec((count, depth), lambda i, at: (0, 0)),
            ]
            + [pl.BlockSpec(memory_space=pl.ANY)] * 8,
            out_specs=pl.BlockSpec((count, YH * sh), lambda i, at: (0, 0)),
            scratch_shapes=[
                pltpu.VMEM((count, depth), jnp.bfloat16),
                pltpu.VMEM((YH, 16 * rows, 2 * sh), jnp.bfloat16),
                pltpu.SemaphoreType.DMA((32,)),
            ],
        ),
        out_shape=jax.ShapeDtypeStruct((count, YH * sh), jnp.bfloat16),
        name="hidden_block",
    )(at, one_hot, seen, text, *pieces)


def expert_kernel(
    at_ref, a_ref, b_ref, t_ref, s_ref, f_ref, g0, u0, g1, u1, moe_ref, o_ref, n_ref, h_ref, d_ref, sems
):
    step, last = pl.program_id(0), pl.num_programs(0) - 1
    side, wide = g0.shape
    hid = d_ref.shape[2]
    copies = [
        pltpu.make_async_copy(moe_ref.at[:, (3 * i + 2) * hid : (3 * i + 3) * hid], d_ref.at[i], sems.at[i])
        for i in range(2)
    ]

    @pl.when(step == 0)
    def _():
        for copy in copies:
            copy.start()
        rows = jnp.dot(a_ref[...], t_ref[...], preferred_element_type=jnp.float32)
        rows += jnp.dot(b_ref[...], s_ref[...], preferred_element_type=jnp.float32)
        n_ref[...] = rows.astype(n_ref.dtype)

    here = pl.ds(pl.multiple_of(at_ref[0] * side, side), side)
    there = pl.ds(pl.multiple_of((1 - at_ref[0]) * side, side), side)
    both = jnp.dot(
        n_ref[:, here],
        jnp.concatenate([g0[...], u0[...]], axis=1),
        preferred_element_type=jnp.float32,
    ) + jnp.dot(
        n_ref[:, there],
        jnp.concatenate([g1[...], u1[...]], axis=1),
        preferred_element_type=jnp.float32,
    )
    h_ref[:, pl.ds(pl.multiple_of(step * wide, wide), wide)] = (
        jax.nn.silu(both[:, :wide]) * both[:, wide:]
    ).astype(h_ref.dtype)

    @pl.when(step == last)
    def _():
        for i, at in enumerate((here, there)):
            copies[i].wait()
            value = lax.dot_general(
                h_ref[...], d_ref[i], (((1,), (1,)), ((), ())), preferred_element_type=jnp.float32
            )
            o_ref[:, at] = (value * f_ref[...]).astype(o_ref.dtype)


def expert_block(low, pick_text, pick_seen, text, seen, factor, moe, hid):
    side, wide, depth = moe.shape[0], 128, text.shape[1]
    count, steps = pick_text.shape[0], hid // 128

    def whole(a):
        return pl.BlockSpec(a.shape, lambda i, at: (0, 0))

    def columns(n):
        return pl.BlockSpec((side, wide), lambda i, at: (0, n * steps + i))

    return pl.pallas_call(
        expert_kernel,
        grid_spec=pltpu.PrefetchScalarGridSpec(
            num_scalar_prefetch=1,
            grid=(steps,),
            in_specs=[whole(a) for a in (pick_text, pick_seen, text, seen, factor)]
            + [columns(n) for n in (0, 1, 3, 4)]
            + [pl.BlockSpec(memory_space=pl.ANY)],
            out_specs=pl.BlockSpec((count, depth), lambda i, at: (0, 0)),
            scratch_shapes=[
                pltpu.VMEM((count, depth), jnp.bfloat16),
                pltpu.VMEM((count, hid), jnp.bfloat16),
                pltpu.VMEM((2, side, hid), jnp.bfloat16),
                pltpu.SemaphoreType.DMA((2,)),
            ],
        ),
        out_shape=jax.ShapeDtypeStruct((count, depth), jnp.bfloat16),
        name="expert_block",
    )(low, pick_text, pick_seen, text, seen, factor, moe, moe, moe, moe, moe)


def down_kernel(first, back, at_ref, h_ref, t_ref, v_ref, u_ref, *refs):
    pieces, o_refs, (w_ref, sems) = refs[:8], refs[8:-2], refs[-2:]
    sh = w_ref.shape[2]
    step = pl.program_id(0)

    @pl.when(step == 0)
    def _():
        for copy in place_pieces(at_ref, pieces, slice(2 * sh, 3 * sh), w_ref, sems):
            copy.wait()

    tok = h_ref.shape[0]
    owner = lax.rem(at_ref[3] - (first - back * step) + X, X) * YH + at_ref[4]
    where = owner * tok + lax.broadcasted_iota(jnp.int32, (tok, t_ref.shape[1]), 0)
    total = jnp.zeros(o_refs[0].shape, jnp.float32)
    for e, values in enumerate((v_ref, u_ref)):
        put = jnp.where(where == t_ref[e : e + 1, :], 1.0, 0.0).astype(jnp.bfloat16)
        total += jnp.dot(put, values[...], preferred_element_type=jnp.float32)
    for b in range(YH):
        total += lax.dot_general(
            h_ref[:, b * sh : (b + 1) * sh],
            w_ref[b],
            (((1,), (1,)), ((), ())),
            preferred_element_type=jnp.float32,
        )
    for n, o_ref in enumerate(o_refs):

        @pl.when(step == n)
        def _():
            o_ref[...] = total.astype(o_ref.dtype)


def down_block(first, back, at, hidden, token_at, values, values_other, pieces):
    _, rows, cols = pieces[0].shape
    sh = cols // 3
    tok, depth = hidden.shape[0] // X, values.shape[1]
    return pl.pallas_call(
        functools.partial(down_kernel, first, back),
        grid_spec=pltpu.PrefetchScalarGridSpec(
            num_scalar_prefetch=1,
            grid=(2,),
            in_specs=[
                pl.BlockSpec((tok, hidden.shape[1]), lambda i, at: (first - back * i, 0)),
                pl.BlockSpec(token_at.shape, lambda i, at: (0, 0)),
                pl.BlockSpec(values.shape, lambda i, at: (0, 0)),
                pl.BlockSpec(values.shape, lambda i, at: (0, 0)),
            ]
            + [pl.BlockSpec(memory_space=pl.ANY)] * 8,
            out_specs=[pl.BlockSpec((tok, depth), lambda i, at: (0, 0))] * 2,
            scratch_shapes=[
                pltpu.VMEM((YH, 16 * rows, sh), jnp.bfloat16),
                pltpu.SemaphoreType.DMA((32,)),
            ],
        ),
        out_shape=[jax.ShapeDtypeStruct((tok, depth), jnp.bfloat16)] * 2,
        name="down_block",
    )(at, hidden, token_at, values, values_other, *pieces)


def vit_kernel(at_ref, n_ref, w_ref, *o_refs):
    wide = w_ref.shape[2] // 2
    total = jnp.zeros(n_ref.shape, jnp.float32)
    for b in range(YH):
        h = jnp.dot(n_ref[...], w_ref[b, :, :wide], preferred_element_type=jnp.float32)
        h = jax.nn.gelu(h, approximate=True).astype(jnp.bfloat16)
        total += lax.dot_general(
            h, w_ref[b, :, wide:], (((1,), (1,)), ((), ())), preferred_element_type=jnp.float32
        )
    for n, o_ref in enumerate(o_refs):

        @pl.when(pl.program_id(0) == n)
        def _():
            o_ref[...] = total.astype(o_ref.dtype)


def vit_block(at, normed, vit):
    rows, width = normed.shape
    step, n = rows // X, at.shape[0]
    return pl.pallas_call(
        vit_kernel,
        grid_spec=pltpu.PrefetchScalarGridSpec(
            num_scalar_prefetch=1,
            grid=(n,),
            in_specs=[
                pl.BlockSpec((step, width), lambda i, at: (at[i], 0)),
                pl.BlockSpec(vit.shape, lambda i, at: (0, 0, 0)),
            ],
            out_specs=[pl.BlockSpec((step, width), lambda i, at: (0, 0))] * n,
        ),
        out_shape=[jax.ShapeDtypeStruct((step, width), jnp.bfloat16)] * n,
        name="vit_block",
    )(at, normed, vit)


def seen_kernel(at_ref, *refs):
    parts, (gain_ref, whole_ref, seen_ref) = refs[: 2 * X], refs[2 * X :]
    rows, cols = parts[0].shape
    for y in range(YH):
        here = pl.ds(y * rows, rows)
        square = 0.0
        for k in range(X):
            part = parts[y * X + k][...].astype(jnp.float32)
            square += jnp.sum(part * part, axis=-1, keepdims=True)
        scale = lax.rsqrt(square / (X * cols) + rms_epsilon)
        for k in range(X):
            x = lax.rem(at_ref[3] - k + X, X)
            at = pl.ds(pl.multiple_of(x * cols, cols), cols)
            part = parts[y * X + k][...]
            whole_ref[here, at] = part
            seen_ref[here, at] = (part.astype(jnp.float32) * scale * gain_ref[:, at]).astype(
                seen_ref.dtype
            )


def seen_block(at, parts, gain):
    rows, cols = parts[0].shape
    shape = (YH * rows, X * cols)
    return pl.pallas_call(
        seen_kernel,
        grid_spec=pltpu.PrefetchScalarGridSpec(
            num_scalar_prefetch=1,
            grid=(1,),
            in_specs=[pl.BlockSpec((rows, cols), lambda i, at: (0, 0))] * len(parts)
            + [pl.BlockSpec((1, X * cols), lambda i, at: (0, 0))],
            out_specs=[pl.BlockSpec(shape, lambda i, at: (0, 0))] * 2,
        ),
        out_shape=[jax.ShapeDtypeStruct(shape, jnp.bfloat16)] * 2,
        name="seen_block",
    )(at, *parts, gain[None])


def text_kernel(*refs):
    parts, (gain_ref, keep_ref, o_ref) = refs[:-3], refs[-3:]
    rows = parts[0].shape[0]
    for n, ref in enumerate(parts):
        part = ref[...].astype(jnp.float32)
        square = jnp.mean(part * part, axis=-1, keepdims=True)
        part = part * lax.rsqrt(square + rms_epsilon) * gain_ref[...]
        here = pl.ds(n * rows, rows)
        o_ref[here, :] = (part * keep_ref[here, :]).astype(o_ref.dtype)


def text_block(parts, gain, keep):
    rows, depth = parts[0].shape
    shape = (rows * len(parts), depth)
    return pl.pallas_call(
        text_kernel,
        out_shape=jax.ShapeDtypeStruct(shape, jnp.bfloat16),
        name="text_block",
    )(*parts, gain[None], keep)


def shards(
    patches,
    counts,
    starts,
    embeds,
    route_ids,
    route_weights,
    vit_gain,
    vit_fc1,
    vit_fc2,
    proj_gain,
    proj_weight,
    moe_gain,
    shared_gate,
    shared_up,
    shared_down,
    expert_gate,
    expert_up,
    expert_down,
):
    xi, yi = lax.axis_index("x"), lax.axis_index("yh")
    rows, width = patches.shape[1], patches.shape[2]
    half = rows // YH
    tok_dev = embeds.shape[1]
    seq_len = tok_dev * X * YH
    vtok = rows // 4
    capacity = seq_len // 8

    def padded(w):
        return jnp.pad(w, ((0, 0), (0, -w.shape[1] % 128)))

    vit_own = jnp.concatenate([padded(vit_fc1), padded(vit_fc2)], axis=1)
    wide = vit_own.shape[1] // 2
    vit = lax.all_gather(vit_own, ("yh",) + FSDP, axis=0, tiled=True).reshape(YH, -1, 2 * wide)
    experts = jnp.concatenate([expert_gate[:, 0], expert_up[:, 0], expert_down[:, 0]], axis=1)
    partner = lax.ppermute(experts, "yl", [(0, 1), (1, 0)])
    moe = lax.all_gather(
        jnp.concatenate([experts, partner], axis=1), ("z", "c"), axis=0, tiled=True
    )
    hid = expert_gate.shape[2]

    own = embeds[0]
    near = [own] + [shift(own, k, 0) for k in range(1, X)]
    other = shift(own, 0, 1)
    far = [other] + [shift(other, k, 0) for k in range(1, X)]
    proj = jnp.stack(ring(proj_weight, "z"))
    shared_own = [padded(shared_gate), padded(shared_up), padded(shared_down)]
    shared_own = jnp.concatenate(shared_own, axis=1)
    shared = jnp.stack(ring(shared_own, "z"))
    place_at = jnp.stack(
        [lax.axis_index("z"), yi * YH + lax.axis_index("yl"), lax.axis_index("c"), xi, yi]
    ).astype(jnp.int32)

    image_rows = lax.dynamic_slice_in_dim(patches[0], yi * half, half, 0)
    normed = layer_norm(image_rows.astype(jnp.float32), vit_gain).astype(jnp.bfloat16)
    vit, normed, proj, shared = tie(vit, normed, proj, shared)
    ahead = vit_block(jnp.stack([(xi + 2) % X, (xi + 1) % X]).astype(jnp.int32), normed, vit)
    got = [shift(ahead[0], 2, 0), shift(ahead[1], 1, 0)]
    rest = vit_block(jnp.stack([(xi + 3) % X, xi]).astype(jnp.int32), normed, vit)
    got += [shift(rest[0], 3, 0)]
    rest, proj, shared = tie(rest, proj, shared)
    proj = ring(proj, ("yh", "yl"))
    shared = ring(shared, ("yh", "yl"))
    mixed = rest[1].astype(jnp.float32)
    for part in got:
        mixed = mixed + part.astype(jnp.float32)
    mine = lax.dynamic_slice_in_dim(patches[0], yi * half + xi * (half // X), half // X, 0)
    residual = mine.astype(jnp.float32) + mixed
    proj_in = layer_norm(residual.reshape(-1, 4 * width), proj_gain).astype(jnp.bfloat16)
    some = proj_in.shape[0] // 2
    left, right = shift(proj_in, 1, 0), shift(proj_in, -1, 0)
    left, right, proj = tie(left, right, proj)
    parts = [proj_in, left, right, shift(left[:some], 1, 0), shift(right[some:], -1, 0)]
    proj = proj + swap_cores(proj)
    visual = proj_block(place_at, parts, proj)
    parts = [visual] + [shift(visual, k, 0) for k in range(1, X)]
    parts = parts + [shift(a, 0, 1) for a in parts]
    whole, seen = seen_block(place_at, parts, moe_gain)
    whole, shared = tie(whole, shared)
    shared = shared + swap_cores(shared)

    where = visual_positions(counts[0], starts[0], vtok)
    where = jnp.where(yi == 0, where, jnp.roll(where, vtok // YH))

    row = jnp.arange(seq_len, dtype=jnp.int32)
    row_x = (xi - row // tok_dev % X) % X
    row_y = (yi - row // (tok_dev * X)) % YH
    row_pos = (row_x * YH + row_y) * tok_dev + row % tok_dev
    take = row_pos[:, None] == where[None, :]
    is_visual = jnp.any(take, axis=1)
    rows_here = tok_dev * X

    text = text_block(near + far, moe_gain, jnp.where(is_visual, 0.0, 1.0)[:, None])
    one_hot = take[:rows_here].astype(jnp.bfloat16)
    merged = jnp.where(
        is_visual[:tok_dev, None], dot(one_hot[:tok_dev], whole), own.astype(jnp.float32)
    )

    def ranks(expert):
        hit = route_ids[0] == expert
        chosen = jnp.any(hit, axis=1)
        share = jnp.sum(jnp.where(hit, route_weights[0], 0.0), axis=1)
        return jnp.where(chosen, jnp.cumsum(chosen.astype(jnp.int32)) - 1, -1), share

    slots = jnp.arange(capacity, dtype=jnp.int32)

    def routed(expert):
        rank, share = ranks(expert)
        place = rank[:, None] == slots[None, :]
        factor = jnp.sum(jnp.where(place, share[:, None], 0.0), axis=0)
        token_at = jnp.sum(jnp.where(place, row[:, None] + 1, 0), axis=0) - 1
        return token_at, factor

    token_at, factor = routed(xi * YH + yi)
    token_at_other, _ = routed(xi * YH + (yi + 1) % YH)
    pick_text = (token_at[:, None] == row_pos[None, :]).astype(jnp.bfloat16)
    pick_seen = (token_at[:, None] == where[None, :]).astype(jnp.bfloat16)
    low = lax.axis_index("yl").astype(jnp.int32)[None]
    values = expert_block(low, pick_text, pick_seen, text, seen, factor[:, None], moe, hid)
    values_other = shift(values, 0, 1)
    hidden = hidden_block(place_at, one_hot, seen, text, shared)
    args = (place_at, hidden, jnp.stack([token_at, token_at_other]), values, values_other, shared)
    far_sum, next_sum = down_block(2, 1, *args)
    sums = [shift(far_sum, -2, 0), shift(next_sum, -1, 0)]
    back_sum, own_sum = down_block(3, 3, *args)
    sums += [shift(back_sum, -3, 0)]
    total = merged + own_sum.astype(jnp.float32)
    for part in sums:
        total = total + part.astype(jnp.float32)
    return total.astype(jnp.bfloat16)[None]


def solution(mesh):
    fine = Mesh(mesh.devices.reshape(X, YH, 2, 4, 2), SEQ + FSDP)
    placed = (
        P(FSDP, None, None),
        P(FSDP, None),
        P(FSDP, None),
        P(FSDP, SEQ, None),
        P(FSDP, None, None),
        P(FSDP, None, None),
        P(),
        P(FSDP, SEQ),
        P(FSDP, SEQ),
        P(),
        P(FSDP, SEQ),
        P(),
        P(FSDP, SEQ),
        P(FSDP, SEQ),
        P(FSDP, SEQ),
        P(FSDP, SEQ, None),
        P(FSDP, SEQ, None),
        P(FSDP, SEQ, None),
    )

    return jax.shard_map(
        shards, mesh=fine, in_specs=placed, out_specs=P(FSDP, SEQ, None), check_vma=False
    )
```

```python
import functools

import jax
import jax.numpy as jnp
from jax import lax
from jax.experimental import pallas as pl
from jax.experimental.pallas import tpu as pltpu
from jax.sharding import Mesh, PartitionSpec as P

ln_epsilon = 1e-05
rms_epsilon = 1e-06
X, YH = 4, 2
FSDP = ("yl", "z", "c")
SEQ = ("x", "yh")


def layer_norm(values, gain_vec):
    center = values - jnp.mean(values, axis=-1, keepdims=True)
    spread = jnp.mean(center * center, axis=-1, keepdims=True)
    return center * lax.rsqrt(spread + ln_epsilon) * gain_vec


def visual_positions(counts, starts, total):
    end_index = jnp.cumsum(counts)
    begins = end_index - counts
    token_index = jnp.arange(total, dtype=jnp.int32)
    inside = (token_index[:, None] >= begins[None, :]) & (token_index[:, None] < end_index[None, :])
    placed = starts[None, :] + token_index[:, None] - begins[None, :]
    return jnp.sum(jnp.where(inside, placed, 0), axis=1)


def shift(a, kx, ky):
    pairs = []
    for i in range(X):
        for j in range(YH):
            pairs.append((i * YH + j, ((i + kx) % X) * YH + (j + ky) % YH))
    return lax.ppermute(a, SEQ, pairs)


def dot(a, b):
    return jnp.dot(a, b, preferred_element_type=jnp.float32)


def tie(*arrays):
    return lax.optimization_barrier(arrays)


def hops(a, axes, steps):
    n = lax.axis_size(axes)
    return [lax.ppermute(a, axes, [(i, (i + k) % n) for i in range(n)]) for k in steps]


def ring(a, axes):
    return [a] + hops(a, axes, range(1, lax.axis_size(axes)))


def swap_cores(pieces):
    return [lax.ppermute(a, "c", [(0, 1), (1, 0)]) for a in pieces]


def place_pieces(at_ref, pieces, columns, w_ref, sems):
    z_own, y_own, c_own = at_ref[0], at_ref[1], at_ref[2]
    copies = []
    for n, piece in enumerate(pieces):
        c = lax.rem(c_own + n // 4, 2)
        y = lax.rem(y_own - n % 4 + 4, 4)
        for k in range(piece.shape[0]):
            z = lax.rem(z_own - k + 4, 4)
            f = lax.rem(y, YH) * 8 + z * 2 + c
            rows = piece.shape[1]
            copies.append(
                pltpu.make_async_copy(
                    piece.at[k, :, columns],
                    w_ref.at[y // YH, pl.ds(pl.multiple_of(f * rows, rows), rows), :],
                    sems.at[n * 4 + k],
                )
            )
    for copy in copies:
        copy.start()
    return copies


def proj_kernel(at_ref, *refs):
    parts, pieces, (o_ref, a_ref, w_ref, sems) = refs[:8], refs[8:16], refs[16:]
    copies = place_pieces(at_ref, pieces, slice(None), w_ref, sems)
    some = parts[0].shape[0]
    for n, back in enumerate((0, 1, X - 1, 2)):
        x = lax.rem(at_ref[3] - back + X, X)
        for i in range(2):
            here = pl.ds(pl.multiple_of((2 * x + i) * some, some), some)
            a_ref[here, :] = parts[2 * n + i][...]
    for copy in copies:
        copy.wait()
    cols = w_ref.shape[2]
    for b in range(YH):
        o_ref[:, b * cols : (b + 1) * cols] = jnp.dot(
            a_ref[...], w_ref[b], preferred_element_type=jnp.float32
        ).astype(o_ref.dtype)


def proj_block(at, parts, pieces):
    _, rows, cols = pieces[0].shape
    count, depth = parts[0].shape
    return pl.pallas_call(
        proj_kernel,
        grid_spec=pltpu.PrefetchScalarGridSpec(
            num_scalar_prefetch=1,
            grid=(1,),
            in_specs=[pl.BlockSpec(a.shape, lambda i, at: (0, 0)) for a in parts]
            + [pl.BlockSpec(memory_space=pl.ANY)] * 8,
            out_specs=pl.BlockSpec((2 * X * count, YH * cols), lambda i, at: (0, 0)),
            scratch_shapes=[
                pltpu.VMEM((2 * X * count, depth), jnp.bfloat16),
                pltpu.VMEM((YH, 16 * rows, cols), jnp.bfloat16),
                pltpu.SemaphoreType.DMA((32,)),
            ],
        ),
        out_shape=jax.ShapeDtypeStruct((2 * X * count, YH * cols), jnp.bfloat16),
        name="proj_block",
    )(at, *parts, *pieces)


def hidden_kernel(at_ref, p_ref, s_ref, t_ref, *refs):
    pieces, (o_ref, n_ref, w_ref, sems) = refs[:8], refs[8:]
    sh = w_ref.shape[2] // 2
    copies = place_pieces(at_ref, pieces, slice(0, 2 * sh), w_ref, sems)
    seen = jnp.dot(p_ref[...], s_ref[...], preferred_element_type=jnp.float32)
    n_ref[...] = seen.astype(n_ref.dtype) + t_ref[...]
    for copy in copies:
        copy.wait()
    for b in range(YH):
        gate = jnp.dot(n_ref[...], w_ref[b, :, :sh], preferred_element_type=jnp.float32)
        up = jnp.dot(n_ref[...], w_ref[b, :, sh:], preferred_element_type=jnp.float32)
        o_ref[:, b * sh : (b + 1) * sh] = (jax.nn.silu(gate) * up).astype(o_ref.dtype)


def hidden_block(at, one_hot, seen, text, pieces):
    _, rows, cols = pieces[0].shape
    sh = cols // 3
    count, depth = one_hot.shape[0], seen.shape[1]
    return pl.pallas_call(
        hidden_kernel,
        grid_spec=pltpu.PrefetchScalarGridSpec(
            num_scalar_prefetch=1,
            grid=(1,),
            in_specs=[
                pl.BlockSpec(one_hot.shape, lambda i, at: (0, 0)),
                pl.BlockSpec(seen.shape, lambda i, at: (0, 0)),
                pl.BlockSpec((count, depth), lambda i, at: (0, 0)),
            ]
            + [pl.BlockSpec(memory_space=pl.ANY)] * 8,
            out_specs=pl.BlockSpec((count, YH * sh), lambda i, at: (0, 0)),
            scratch_shapes=[
                pltpu.VMEM((count, depth), jnp.bfloat16),
                pltpu.VMEM((YH, 16 * rows, 2 * sh), jnp.bfloat16),
                pltpu.SemaphoreType.DMA((32,)),
            ],
        ),
        out_shape=jax.ShapeDtypeStruct((count, YH * sh), jnp.bfloat16),
        name="hidden_block",
    )(at, one_hot, seen, text, *pieces)


def expert_kernel(at_ref, a_ref, b_ref, t_ref, s_ref, f_ref, moe_ref, o_ref, n_ref, w_ref, sems):
    _, side, hid = w_ref.shape
    copies = []
    for n, i in enumerate((0, 1, 3, 4, 2, 5)):
        copies.append(
            pltpu.make_async_copy(moe_ref.at[:, i * hid : (i + 1) * hid], w_ref.at[n], sems.at[n])
        )
    for copy in copies:
        copy.start()
    rows = jnp.dot(a_ref[...], t_ref[...], preferred_element_type=jnp.float32)
    rows += jnp.dot(b_ref[...], s_ref[...], preferred_element_type=jnp.float32)
    n_ref[...] = rows.astype(n_ref.dtype)
    here = pl.ds(pl.multiple_of(at_ref[0] * side, side), side)
    there = pl.ds(pl.multiple_of((1 - at_ref[0]) * side, side), side)
    sums = [0.0, 0.0]
    for n in range(4):
        copies[n].wait()
        part = n_ref[:, here if n < 2 else there]
        sums[n % 2] += jnp.dot(part, w_ref[n], preferred_element_type=jnp.float32)
    hidden = (jax.nn.silu(sums[0]) * sums[1]).astype(n_ref.dtype)
    for n, at in ((4, here), (5, there)):
        copies[n].wait()
        value = lax.dot_general(
            hidden, w_ref[n], (((1,), (1,)), ((), ())), preferred_element_type=jnp.float32
        )
        o_ref[:, at] = (value * f_ref[...]).astype(o_ref.dtype)


def expert_block(low, pick_text, pick_seen, text, seen, factor, moe, hid):
    side, depth = moe.shape[0], text.shape[1]
    count = pick_text.shape[0]

    def whole(a):
        return pl.BlockSpec(a.shape, lambda i, at: (0, 0))

    return pl.pallas_call(
        expert_kernel,
        grid_spec=pltpu.PrefetchScalarGridSpec(
            num_scalar_prefetch=1,
            grid=(1,),
            in_specs=[whole(a) for a in (pick_text, pick_seen, text, seen, factor)]
            + [pl.BlockSpec(memory_space=pl.ANY)],
            out_specs=pl.BlockSpec((count, depth), lambda i, at: (0, 0)),
            scratch_shapes=[
                pltpu.VMEM((count, depth), jnp.bfloat16),
                pltpu.VMEM((6, side, hid), jnp.bfloat16),
                pltpu.SemaphoreType.DMA((6,)),
            ],
        ),
        out_shape=jax.ShapeDtypeStruct((count, depth), jnp.bfloat16),
        name="expert_block",
    )(low, pick_text, pick_seen, text, seen, factor, moe)


def down_kernel(blocks, at_ref, h_ref, t_ref, v_ref, u_ref, *refs):
    pieces, o_refs, (w_ref, sems) = refs[:8], refs[8:-2], refs[-2:]
    sh, tok = w_ref.shape[2], o_refs[0].shape[0]
    copies = place_pieces(at_ref, pieces, slice(2 * sh, 3 * sh), w_ref, sems)
    lanes = lax.broadcasted_iota(jnp.int32, (tok, t_ref.shape[1]), 0)
    where = jnp.concatenate(
        [(lax.rem(at_ref[3] - k + X, X) * YH + at_ref[4]) * tok + lanes for k in blocks], axis=0
    )
    total = 0.0
    for e, values in enumerate((v_ref, u_ref)):
        put = jnp.where(where == t_ref[e : e + 1, :], 1.0, 0.0).astype(jnp.bfloat16)
        total += jnp.dot(put, values[...], preferred_element_type=jnp.float32)
    hidden = jnp.concatenate([h_ref[k * tok : (k + 1) * tok, :] for k in blocks], axis=0)
    for copy in copies:
        copy.wait()
    for b in range(YH):
        total += lax.dot_general(
            hidden[:, b * sh : (b + 1) * sh],
            w_ref[b],
            (((1,), (1,)), ((), ())),
            preferred_element_type=jnp.float32,
        )
    for n, o_ref in enumerate(o_refs):
        o_ref[...] = total[n * tok : (n + 1) * tok].astype(o_ref.dtype)


def down_block(blocks, at, hidden, token_at, values, values_other, pieces):
    _, rows, cols = pieces[0].shape
    sh = cols // 3
    tok, depth = hidden.shape[0] // X, values.shape[1]

    def whole(a):
        return pl.BlockSpec(a.shape, lambda i, at: (0, 0))

    return pl.pallas_call(
        functools.partial(down_kernel, blocks),
        grid_spec=pltpu.PrefetchScalarGridSpec(
            num_scalar_prefetch=1,
            grid=(1,),
            in_specs=[whole(a) for a in (hidden, token_at, values, values_other)]
            + [pl.BlockSpec(memory_space=pl.ANY)] * 8,
            out_specs=[pl.BlockSpec((tok, depth), lambda i, at: (0, 0))] * len(blocks),
            scratch_shapes=[
                pltpu.VMEM((YH, 16 * rows, sh), jnp.bfloat16),
                pltpu.SemaphoreType.DMA((32,)),
            ],
        ),
        out_shape=[jax.ShapeDtypeStruct((tok, depth), jnp.bfloat16)] * len(blocks),
        name="down_block",
    )(at, hidden, token_at, values, values_other, *pieces)


def vit_kernel(at_ref, n_ref, w_ref, *o_refs):
    wide = w_ref.shape[2] // 2
    total = jnp.zeros(n_ref.shape, jnp.float32)
    for b in range(YH):
        h = jnp.dot(n_ref[...], w_ref[b, :, :wide], preferred_element_type=jnp.float32)
        h = jax.nn.gelu(h, approximate=True).astype(jnp.bfloat16)
        total += lax.dot_general(
            h, w_ref[b, :, wide:], (((1,), (1,)), ((), ())), preferred_element_type=jnp.float32
        )
    for n, o_ref in enumerate(o_refs):

        @pl.when(pl.program_id(0) == n)
        def _():
            o_ref[...] = total.astype(o_ref.dtype)


def vit_block(at, normed, vit):
    rows, width = normed.shape
    step, n = rows // X, at.shape[0]
    return pl.pallas_call(
        vit_kernel,
        grid_spec=pltpu.PrefetchScalarGridSpec(
            num_scalar_prefetch=1,
            grid=(n,),
            in_specs=[
                pl.BlockSpec((step, width), lambda i, at: (at[i], 0)),
                pl.BlockSpec(vit.shape, lambda i, at: (0, 0, 0)),
            ],
            out_specs=[pl.BlockSpec((step, width), lambda i, at: (0, 0))] * n,
        ),
        out_shape=[jax.ShapeDtypeStruct((step, width), jnp.bfloat16)] * n,
        name="vit_block",
    )(at, normed, vit)


def seen_kernel(at_ref, *refs):
    parts, (gain_ref, whole_ref, seen_ref) = refs[: 2 * X], refs[2 * X :]
    rows, cols = parts[0].shape
    for y in range(YH):
        here = pl.ds(y * rows, rows)
        square = 0.0
        for k in range(X):
            part = parts[y * X + k][...].astype(jnp.float32)
            square += jnp.sum(part * part, axis=-1, keepdims=True)
        scale = lax.rsqrt(square / (X * cols) + rms_epsilon)
        for k in range(X):
            x = lax.rem(at_ref[3] - k + X, X)
            at = pl.ds(pl.multiple_of(x * cols, cols), cols)
            part = parts[y * X + k][...]
            whole_ref[here, at] = part
            seen_ref[here, at] = (part.astype(jnp.float32) * scale * gain_ref[:, at]).astype(
                seen_ref.dtype
            )


def seen_block(at, parts, gain):
    rows, cols = parts[0].shape
    shape = (YH * rows, X * cols)
    return pl.pallas_call(
        seen_kernel,
        grid_spec=pltpu.PrefetchScalarGridSpec(
            num_scalar_prefetch=1,
            grid=(1,),
            in_specs=[pl.BlockSpec((rows, cols), lambda i, at: (0, 0))] * len(parts)
            + [pl.BlockSpec((1, X * cols), lambda i, at: (0, 0))],
            out_specs=[pl.BlockSpec(shape, lambda i, at: (0, 0))] * 2,
        ),
        out_shape=[jax.ShapeDtypeStruct(shape, jnp.bfloat16)] * 2,
        name="seen_block",
    )(at, *parts, gain[None])


def join_kernel(at_ref, p_ref, a0, a1, a2, a3, gain_ref, top_ref, low_ref, s_ref):
    mixed = a0[...].astype(jnp.float32)
    for ref in (a1, a2, a3):
        mixed += ref[...].astype(jnp.float32)
    mixed = p_ref[...].astype(jnp.float32) + mixed
    tiles, rows, lanes = s_ref.shape
    for t in range(tiles):
        s_ref[t] = mixed[:, t * lanes : (t + 1) * lanes]
    width, count, some = tiles * lanes, rows // 4, top_ref.shape[0]
    parts = [
        jnp.concatenate([s_ref[t, pl.ds(p, count, stride=4), :] for t in range(tiles)], axis=1)
        for p in range(4)
    ]
    mean = sum(jnp.sum(part, axis=-1, keepdims=True) for part in parts) / (4 * width)
    parts = [part - mean for part in parts]
    square = sum(jnp.sum(part * part, axis=-1, keepdims=True) for part in parts) / (4 * width)
    scale = lax.rsqrt(square + ln_epsilon)
    for p, part in enumerate(parts):
        here = slice(p * width, (p + 1) * width)
        out = (part * scale * gain_ref[:, here]).astype(top_ref.dtype)
        top_ref[:, here] = out[:some]
        low_ref[:, here] = out[some:]


def join_block(at, patches, parts, gain):
    rows, width = parts[0].shape
    shape = (rows // 8, 4 * width)

    def whole(*size):
        return pl.BlockSpec(size, lambda i, at: (0, 0))

    return pl.pallas_call(
        join_kernel,
        grid_spec=pltpu.PrefetchScalarGridSpec(
            num_scalar_prefetch=1,
            grid=(1,),
            in_specs=[pl.BlockSpec((rows, width), lambda i, at: (at[4] * X + at[3], 0))]
            + [whole(rows, width)] * 4
            + [whole(1, 4 * width)],
            out_specs=[whole(*shape)] * 2,
            scratch_shapes=[pltpu.VMEM((width // 128, rows, 128), jnp.float32)],
        ),
        out_shape=[jax.ShapeDtypeStruct(shape, jnp.bfloat16)] * 2,
        name="join_block",
    )(at, patches, *parts, gain[None])


def text_kernel(*refs):
    parts, (gain_ref, keep_ref, o_ref) = refs[:-3], refs[-3:]
    rows = parts[0].shape[0]
    for n, ref in enumerate(parts):
        part = ref[...].astype(jnp.float32)
        square = jnp.mean(part * part, axis=-1, keepdims=True)
        part = part * lax.rsqrt(square + rms_epsilon) * gain_ref[...]
        here = pl.ds(n * rows, rows)
        o_ref[here, :] = (part * keep_ref[here, :]).astype(o_ref.dtype)


def text_block(parts, gain, keep):
    rows, depth = parts[0].shape
    shape = (rows * len(parts), depth)
    return pl.pallas_call(
        text_kernel,
        out_shape=jax.ShapeDtypeStruct(shape, jnp.bfloat16),
        name="text_block",
    )(*parts, gain[None], keep)


def shards(
    patches,
    counts,
    starts,
    embeds,
    route_ids,
    route_weights,
    vit_gain,
    vit_fc1,
    vit_fc2,
    proj_gain,
    proj_weight,
    moe_gain,
    shared_gate,
    shared_up,
    shared_down,
    expert_gate,
    expert_up,
    expert_down,
):
    xi, yi = lax.axis_index("x"), lax.axis_index("yh")
    rows = patches.shape[1]
    half = rows // YH
    tok_dev = embeds.shape[1]
    seq_len = tok_dev * X * YH
    vtok = rows // 4
    capacity = seq_len // 8

    def padded(w):
        return jnp.pad(w, ((0, 0), (0, -w.shape[1] % 128)))

    vit_own = jnp.concatenate([padded(vit_fc1), padded(vit_fc2)], axis=1)
    wide = vit_own.shape[1] // 2
    vit = lax.all_gather(vit_own, ("yh",) + FSDP, axis=0, tiled=True).reshape(YH, -1, 2 * wide)
    experts = jnp.concatenate([expert_gate[:, 0], expert_up[:, 0], expert_down[:, 0]], axis=1)
    partner = lax.ppermute(experts, "yl", [(0, 1), (1, 0)])
    moe = lax.all_gather(
        jnp.concatenate([experts, partner], axis=1), ("z", "c"), axis=0, tiled=True
    )
    hid = expert_gate.shape[2]

    own = embeds[0]
    near = [own] + [shift(own, k, 0) for k in range(1, X)]
    other = shift(own, 0, 1)
    far = [other] + [shift(other, k, 0) for k in range(1, X)]
    proj = jnp.stack(ring(proj_weight, "z"))
    shared_own = [padded(shared_gate), padded(shared_up), padded(shared_down)]
    shared_own = jnp.concatenate(shared_own, axis=1)
    shared = jnp.stack(ring(shared_own, "z"))
    place_at = jnp.stack(
        [lax.axis_index("z"), yi * YH + lax.axis_index("yl"), lax.axis_index("c"), xi, yi]
    ).astype(jnp.int32)

    image_rows = lax.dynamic_slice_in_dim(patches[0], yi * half, half, 0)
    normed = layer_norm(image_rows.astype(jnp.float32), vit_gain).astype(jnp.bfloat16)
    vit, normed, proj, shared = tie(vit, normed, proj, shared)
    ahead = vit_block(jnp.stack([(xi + 2) % X, (xi + 1) % X]).astype(jnp.int32), normed, vit)
    got = [shift(ahead[0], 2, 0), shift(ahead[1], 1, 0)]
    rest = vit_block(jnp.stack([(xi + 3) % X, xi]).astype(jnp.int32), normed, vit)
    got += [shift(rest[0], 3, 0)]
    rest, proj, shared = tie(rest, proj, shared)
    proj = ring(proj, ("yh", "yl"))
    shared = [shared] + hops(shared, ("yh", "yl"), (1, 3))
    top, bottom = join_block(place_at, patches[0], [rest[1]] + got, proj_gain)
    left_top, right_bottom = shift(top, 1, 0), shift(bottom, -1, 0)
    left_bottom, right_top = shift(bottom, 1, 0), shift(top, -1, 0)
    far_top, far_bottom = shift(left_top, 1, 0), shift(right_bottom, -1, 0)
    left_bottom, right_top, proj = tie(left_bottom, right_top, proj)
    parts = [top, bottom, left_top, left_bottom, right_top, right_bottom, far_top, far_bottom]
    proj = proj + swap_cores(proj)
    visual = proj_block(place_at, parts, proj)
    visual, *shared = tie(visual, *shared)
    partner_visual = shift(visual, 0, 1)
    parts = [visual] + [shift(visual, k, 0) for k in range(1, X)]
    shared += hops(shared[0], ("yh", "yl"), (2,))
    parts += [partner_visual] + [shift(partner_visual, k, 0) for k in range(1, X)]
    swapped = swap_cores(shared[:3])
    whole, seen = seen_block(place_at, parts, moe_gain)
    whole, middle = tie(whole, shared[3])
    swapped += swap_cores([middle])
    own_core = [shared[0], shared[1], middle, shared[2]]
    shared = own_core + [swapped[0], swapped[1], swapped[3], swapped[2]]

    where = visual_positions(counts[0], starts[0], vtok)
    where = jnp.where(yi == 0, where, jnp.roll(where, vtok // YH))

    row = jnp.arange(seq_len, dtype=jnp.int32)
    row_x = (xi - row // tok_dev % X) % X
    row_y = (yi - row // (tok_dev * X)) % YH
    row_pos = (row_x * YH + row_y) * tok_dev + row % tok_dev
    take = row_pos[:, None] == where[None, :]
    is_visual = jnp.any(take, axis=1)
    rows_here = tok_dev * X

    text = text_block(near + far, moe_gain, jnp.where(is_visual, 0.0, 1.0)[:, None])
    one_hot = take[:rows_here].astype(jnp.bfloat16)
    merged = jnp.where(
        is_visual[:tok_dev, None], dot(one_hot[:tok_dev], whole), own.astype(jnp.float32)
    )

    def ranks(expert):
        hit = route_ids[0] == expert
        chosen = jnp.any(hit, axis=1)
        share = jnp.sum(jnp.where(hit, route_weights[0], 0.0), axis=1)
        return jnp.where(chosen, jnp.cumsum(chosen.astype(jnp.int32)) - 1, -1), share

    slots = jnp.arange(capacity, dtype=jnp.int32)

    def routed(expert):
        rank, share = ranks(expert)
        place = rank[:, None] == slots[None, :]
        factor = jnp.sum(jnp.where(place, share[:, None], 0.0), axis=0)
        token_at = jnp.sum(jnp.where(place, row[:, None] + 1, 0), axis=0) - 1
        return token_at, factor

    token_at, factor = routed(xi * YH + yi)
    token_at_other, _ = routed(xi * YH + (yi + 1) % YH)
    pick_text = (token_at[:, None] == row_pos[None, :]).astype(jnp.bfloat16)
    pick_seen = (token_at[:, None] == where[None, :]).astype(jnp.bfloat16)
    low = lax.axis_index("yl").astype(jnp.int32)[None]
    values = expert_block(low, pick_text, pick_seen, text, seen, factor[:, None], moe, hid)
    values_other = shift(values, 0, 1)
    hidden = hidden_block(place_at, one_hot, seen, text, shared)
    args = (place_at, hidden, jnp.stack([token_at, token_at_other]), values, values_other, shared)
    far_sum, next_sum = down_block((2, 1), *args)
    sums = [shift(far_sum, -2, 0), shift(next_sum, -1, 0)]
    back_sum, own_sum = down_block((3, 0), *args)
    sums += [shift(back_sum, -3, 0)]
    total = merged + own_sum.astype(jnp.float32)
    for part in sums:
        total = total + part.astype(jnp.float32)
    return total.astype(jnp.bfloat16)[None]


def solution(mesh):
    fine = Mesh(mesh.devices.reshape(X, YH, 2, 4, 2), SEQ + FSDP)
    placed = (
        P(FSDP, None, None),
        P(FSDP, None),
        P(FSDP, None),
        P(FSDP, SEQ, None),
        P(FSDP, None, None),
        P(FSDP, None, None),
        P(),
        P(FSDP, SEQ),
        P(FSDP, SEQ),
        P(),
        P(FSDP, SEQ),
        P(),
        P(FSDP, SEQ),
        P(FSDP, SEQ),
        P(FSDP, SEQ),
        P(FSDP, SEQ, None),
        P(FSDP, SEQ, None),
        P(FSDP, SEQ, None),
    )

    return jax.shard_map(
        shards, mesh=fine, in_specs=placed, out_specs=P(FSDP, SEQ, None), check_vma=False
    )
```

```python
import jax
import jax.numpy as jnp
from jax import lax
from jax.experimental import pallas as pl
from jax.experimental.pallas import tpu as pltpu
from jax.sharding import Mesh, PartitionSpec as P

ln_epsilon = 1e-05
rms_epsilon = 1e-06
X, YH = 4, 2
FSDP = ("yl", "z", "c")
SEQ = ("x", "yh")


def visual_positions(counts, starts, total):
    end_index = jnp.cumsum(counts)
    begins = end_index - counts
    token_index = jnp.arange(total, dtype=jnp.int32)
    inside = (token_index[:, None] >= begins[None, :]) & (token_index[:, None] < end_index[None, :])
    placed = starts[None, :] + token_index[:, None] - begins[None, :]
    return jnp.sum(jnp.where(inside, placed, 0), axis=1)


def shift(a, kx, ky):
    pairs = []
    for i in range(X):
        for j in range(YH):
            pairs.append((i * YH + j, ((i + kx) % X) * YH + (j + ky) % YH))
    return lax.ppermute(a, SEQ, pairs)


def dot(a, b):
    return jnp.dot(a, b, preferred_element_type=jnp.float32)


def tie(*arrays):
    return lax.optimization_barrier(arrays)


def hops(a, axes, steps):
    n = lax.axis_size(axes)
    return [lax.ppermute(a, axes, [(i, (i + k) % n) for i in range(n)]) for k in steps]


def ring(a, axes):
    return [a] + hops(a, axes, range(1, lax.axis_size(axes)))


def swap_cores(pieces):
    return [lax.ppermute(a, "c", [(0, 1), (1, 0)]) for a in pieces]


def place_pieces(at_ref, pieces, columns, w_ref, sems, act):
    z_own, y_own, c_own = at_ref[0], at_ref[1], at_ref[2]
    for n, piece in enumerate(pieces):
        c = lax.rem(c_own + n // 4, 2)
        y = lax.rem(y_own - n % 4 + 4, 4)
        for k in range(piece.shape[0]):
            z = lax.rem(z_own - k + 4, 4)
            f = lax.rem(y, YH) * 8 + z * 2 + c
            rows = piece.shape[1]
            copy = pltpu.make_async_copy(
                piece.at[k, :, columns],
                w_ref.at[y // YH, pl.ds(pl.multiple_of(f * rows, rows), rows), :],
                sems.at[n * 4 + k],
            )
            copy.start() if act == "start" else copy.wait()


def proj_kernel(at_ref, *refs):
    parts, pieces, (o_ref, a_ref, w_ref, sems) = refs[:8], refs[8:16], refs[16:]
    place_pieces(at_ref, pieces, slice(None), w_ref, sems, "start")
    some = parts[0].shape[0]
    for n, back in enumerate((0, 1, X - 1, 2)):
        x = lax.rem(at_ref[3] - back + X, X)
        for i in range(2):
            here = pl.ds(pl.multiple_of((2 * x + i) * some, some), some)
            a_ref[here, :] = parts[2 * n + i][...]
    place_pieces(at_ref, pieces, slice(None), w_ref, sems, "wait")
    cols = w_ref.shape[2]
    for b in range(YH):
        o_ref[:, b * cols : (b + 1) * cols] = jnp.dot(
            a_ref[...], w_ref[b], preferred_element_type=jnp.float32
        ).astype(o_ref.dtype)


def proj_block(at, parts, pieces):
    _, rows, cols = pieces[0].shape
    count, depth = parts[0].shape
    return pl.pallas_call(
        proj_kernel,
        grid_spec=pltpu.PrefetchScalarGridSpec(
            num_scalar_prefetch=1,
            grid=(1,),
            in_specs=[pl.BlockSpec(a.shape, lambda i, at: (0, 0)) for a in parts]
            + [pl.BlockSpec(memory_space=pl.ANY)] * 8,
            out_specs=pl.BlockSpec((2 * X * count, YH * cols), lambda i, at: (0, 0)),
            scratch_shapes=[
                pltpu.VMEM((2 * X * count, depth), jnp.bfloat16),
                pltpu.VMEM((YH, 16 * rows, cols), jnp.bfloat16),
                pltpu.SemaphoreType.DMA((32,)),
            ],
        ),
        out_shape=jax.ShapeDtypeStruct((2 * X * count, YH * cols), jnp.bfloat16),
    )(at, *parts, *pieces)


def hidden_kernel(at_ref, p_ref, s_ref, t_ref, *refs):
    pieces, (o_ref, n_ref, w_ref, sems) = refs[:8], refs[8:]
    sh = w_ref.shape[2] // 2
    step = pl.program_id(0)

    @pl.when(step == 0)
    def _():
        place_pieces(at_ref, pieces, slice(0, 2 * sh), w_ref, sems, "start")

    seen = jnp.dot(p_ref[...], s_ref[...], preferred_element_type=jnp.float32)
    n_ref[...] = seen.astype(n_ref.dtype) + t_ref[...]

    @pl.when(step == 0)
    def _():
        place_pieces(at_ref, pieces, slice(0, 2 * sh), w_ref, sems, "wait")

    for b in range(YH):
        gate = jnp.dot(n_ref[...], w_ref[b, :, :sh], preferred_element_type=jnp.float32)
        up = jnp.dot(n_ref[...], w_ref[b, :, sh:], preferred_element_type=jnp.float32)
        o_ref[:, b * sh : (b + 1) * sh] = (jax.nn.silu(gate) * up).astype(o_ref.dtype)


def hidden_block(at, one_hot, seen, text, pieces):
    _, rows, cols = pieces[0].shape
    sh = cols // 3
    count, depth = one_hot.shape[0], seen.shape[1]
    some = count // 2
    return pl.pallas_call(
        hidden_kernel,
        grid_spec=pltpu.PrefetchScalarGridSpec(
            num_scalar_prefetch=1,
            grid=(2,),
            in_specs=[
                pl.BlockSpec((some, one_hot.shape[1]), lambda i, at: (i, 0)),
                pl.BlockSpec(seen.shape, lambda i, at: (0, 0)),
                pl.BlockSpec((some, depth), lambda i, at: (i, 0)),
            ]
            + [pl.BlockSpec(memory_space=pl.ANY)] * 8,
            out_specs=pl.BlockSpec((some, YH * sh), lambda i, at: (i, 0)),
            scratch_shapes=[
                pltpu.VMEM((some, depth), jnp.bfloat16),
                pltpu.VMEM((YH, 16 * rows, 2 * sh), jnp.bfloat16),
                pltpu.SemaphoreType.DMA((32,)),
            ],
        ),
        out_shape=jax.ShapeDtypeStruct((count, YH * sh), jnp.bfloat16),
    )(at, one_hot, seen, text, *pieces)


def expert_kernel(
    at_ref, a_ref, b_ref, t_ref, s_ref, f_ref, moe_ref, o_ref, n_ref, g_ref, w_ref, sems
):
    _, side, hid = w_ref.shape
    step = pl.program_id(0)
    copies = []
    for n, i in enumerate((0, 1, 3, 4, 2, 5)):
        copies.append(
            pltpu.make_async_copy(moe_ref.at[:, i * hid : (i + 1) * hid], w_ref.at[n], sems.at[n])
        )

    @pl.when(step == 0)
    def _():
        for copy in copies:
            copy.start()
        rows = jnp.dot(a_ref[...], t_ref[...], preferred_element_type=jnp.float32)
        rows += jnp.dot(b_ref[...], s_ref[...], preferred_element_type=jnp.float32)
        n_ref[...] = rows.astype(n_ref.dtype)
        g_ref[...] = jnp.zeros_like(g_ref)
        copies[0].wait()
        copies[1].wait()

    @pl.when(step == 1)
    def _():
        copies[2].wait()
        copies[3].wait()

    half = lax.rem(at_ref[0] + step, 2)
    part = n_ref[:, pl.ds(pl.multiple_of(half * side, side), side)]
    for n in range(2):
        g_ref[n] += jnp.dot(part, w_ref[2 * step + n], preferred_element_type=jnp.float32)

    @pl.when(step == 1)
    def _():
        hidden = (jax.nn.silu(g_ref[0]) * g_ref[1]).astype(n_ref.dtype)
        copies[4].wait()
        copies[5].wait()

        @pl.loop(0, 2)
        def _(i):
            at = lax.rem(at_ref[0] + i, 2)
            value = lax.dot_general(
                hidden, w_ref[4 + i], (((1,), (1,)), ((), ())), preferred_element_type=jnp.float32
            )
            o_ref[:, pl.ds(pl.multiple_of(at * side, side), side)] = (value * f_ref[...]).astype(
                o_ref.dtype
            )


def expert_block(low, pick_text, pick_seen, text, seen, factor, moe, hid):
    side, depth = moe.shape[0], text.shape[1]
    count = pick_text.shape[0]

    def whole(a):
        return pl.BlockSpec(a.shape, lambda i, at: (0, 0))

    return pl.pallas_call(
        expert_kernel,
        grid_spec=pltpu.PrefetchScalarGridSpec(
            num_scalar_prefetch=1,
            grid=(2,),
            in_specs=[whole(a) for a in (pick_text, pick_seen, text, seen, factor)]
            + [pl.BlockSpec(memory_space=pl.ANY)],
            out_specs=pl.BlockSpec((count, depth), lambda i, at: (0, 0)),
            scratch_shapes=[
                pltpu.VMEM((count, depth), jnp.bfloat16),
                pltpu.VMEM((2, count, hid), jnp.float32),
                pltpu.VMEM((6, side, hid), jnp.bfloat16),
                pltpu.SemaphoreType.DMA((6,)),
            ],
        ),
        out_shape=jax.ShapeDtypeStruct((count, depth), jnp.bfloat16),
    )(low, pick_text, pick_seen, text, seen, factor, moe)


def down_kernel(at_ref, h_ref, t_ref, v_ref, u_ref, *refs):
    pieces, o_refs, (w_ref, sems) = refs[:8], refs[8:-2], refs[-2:]
    sh, tok = w_ref.shape[2], o_refs[0].shape[0]
    place_pieces(at_ref, pieces, slice(2 * sh, 3 * sh), w_ref, sems, "start")
    blocks = [at_ref[5 + n] for n in range(len(o_refs))]
    lanes = lax.broadcasted_iota(jnp.int32, (tok, t_ref.shape[1]), 0)
    where = jnp.concatenate(
        [(lax.rem(at_ref[3] - k + X, X) * YH + at_ref[4]) * tok + lanes for k in blocks], axis=0
    )
    total = 0.0
    for e, values in enumerate((v_ref, u_ref)):
        put = jnp.where(where == t_ref[e : e + 1, :], 1.0, 0.0).astype(jnp.bfloat16)
        total += jnp.dot(put, values[...], preferred_element_type=jnp.float32)
    hidden = jnp.concatenate([h_ref[pl.ds(pl.multiple_of(k * tok, tok), tok), :] for k in blocks], axis=0)
    place_pieces(at_ref, pieces, slice(2 * sh, 3 * sh), w_ref, sems, "wait")
    for b in range(YH):
        total += lax.dot_general(
            hidden[:, b * sh : (b + 1) * sh],
            w_ref[b],
            (((1,), (1,)), ((), ())),
            preferred_element_type=jnp.float32,
        )
    for n, o_ref in enumerate(o_refs):
        o_ref[...] = total[n * tok : (n + 1) * tok].astype(o_ref.dtype)


def down_block(blocks, at, hidden, token_at, values, values_other, pieces):
    at = jnp.concatenate([at, jnp.array(blocks, jnp.int32)])
    _, rows, cols = pieces[0].shape
    sh = cols // 3
    tok, depth = hidden.shape[0] // X, values.shape[1]

    def whole(a):
        return pl.BlockSpec(a.shape, lambda i, at: (0, 0))

    return pl.pallas_call(
        down_kernel,
        grid_spec=pltpu.PrefetchScalarGridSpec(
            num_scalar_prefetch=1,
            grid=(1,),
            in_specs=[whole(a) for a in (hidden, token_at, values, values_other)]
            + [pl.BlockSpec(memory_space=pl.ANY)] * 8,
            out_specs=[pl.BlockSpec((tok, depth), lambda i, at: (0, 0))] * len(blocks),
            scratch_shapes=[
                pltpu.VMEM((YH, 16 * rows, sh), jnp.bfloat16),
                pltpu.SemaphoreType.DMA((32,)),
            ],
        ),
        out_shape=[jax.ShapeDtypeStruct((tok, depth), jnp.bfloat16)] * len(blocks),
    )(at, hidden, token_at, values, values_other, *pieces)


def vit_kernel(at_ref, n_ref, w_ref, *o_refs):
    wide = w_ref.shape[2] // 2
    total = jnp.zeros(n_ref.shape, jnp.float32)
    for b in range(YH):
        h = jnp.dot(n_ref[...], w_ref[b, :, :wide], preferred_element_type=jnp.float32)
        h = jax.nn.gelu(h, approximate=True).astype(jnp.bfloat16)
        total += lax.dot_general(
            h, w_ref[b, :, wide:], (((1,), (1,)), ((), ())), preferred_element_type=jnp.float32
        )
    for n, o_ref in enumerate(o_refs):

        @pl.when(pl.program_id(0) == n)
        def _():
            o_ref[...] = total.astype(o_ref.dtype)


def vit_block(at, normed, vit):
    rows, width = normed.shape
    step, n = rows // X, at.shape[0]
    return pl.pallas_call(
        vit_kernel,
        grid_spec=pltpu.PrefetchScalarGridSpec(
            num_scalar_prefetch=1,
            grid=(n,),
            in_specs=[
                pl.BlockSpec((step, width), lambda i, at: (at[i], 0)),
                pl.BlockSpec(vit.shape, lambda i, at: (0, 0, 0)),
            ],
            out_specs=[pl.BlockSpec((step, width), lambda i, at: (0, 0))] * n,
        ),
        out_shape=[jax.ShapeDtypeStruct((step, width), jnp.bfloat16)] * n,
    )(at, normed, vit)


def seen_kernel(at_ref, *refs):
    parts, (gain_ref, whole_ref, seen_ref) = refs[: 2 * X], refs[2 * X :]
    cols = parts[0].shape[1]
    for y in range(YH):
        square = 0.0
        for k in range(X):
            part = parts[y * X + k][...].astype(jnp.float32)
            square += jnp.sum(part * part, axis=-1, keepdims=True)
        scale = lax.rsqrt(square / (X * cols) + rms_epsilon)
        for k in range(X):
            x = lax.rem(at_ref[3] - k + X, X)
            at = pl.ds(pl.multiple_of(x * cols, cols), cols)
            part = parts[y * X + k][...]
            whole_ref[y, :, at] = part
            seen_ref[y, :, at] = (part.astype(jnp.float32) * scale * gain_ref[:, at]).astype(
                seen_ref.dtype
            )


def seen_block(at, parts, gain):
    rows, cols = parts[0].shape
    steps = 4
    some, depth = rows // steps, X * cols
    outs = pl.pallas_call(
        seen_kernel,
        grid_spec=pltpu.PrefetchScalarGridSpec(
            num_scalar_prefetch=1,
            grid=(steps,),
            in_specs=[pl.BlockSpec((some, cols), lambda i, at: (i, 0))] * len(parts)
            + [pl.BlockSpec((1, depth), lambda i, at: (0, 0))],
            out_specs=[pl.BlockSpec((YH, some, depth), lambda i, at: (0, i, 0))] * 2,
        ),
        out_shape=[jax.ShapeDtypeStruct((YH, rows, depth), jnp.bfloat16)] * 2,
    )(at, *parts, gain[None])
    return [out.reshape(YH * rows, depth) for out in outs]


def norm_kernel(at_ref, p_ref, gain_ref, o_ref):
    rows = p_ref[...].astype(jnp.float32)
    rows = rows - jnp.mean(rows, axis=-1, keepdims=True)
    square = jnp.mean(rows * rows, axis=-1, keepdims=True)
    o_ref[...] = (rows * lax.rsqrt(square + ln_epsilon) * gain_ref[...]).astype(o_ref.dtype)


def norm_block(at, patches, gain):
    rows, width = patches.shape
    steps = 8
    some = rows // YH // steps
    return pl.pallas_call(
        norm_kernel,
        grid_spec=pltpu.PrefetchScalarGridSpec(
            num_scalar_prefetch=1,
            grid=(steps,),
            in_specs=[
                pl.BlockSpec((some, width), lambda i, at: (at[4] * steps + i, 0)),
                pl.BlockSpec((1, width), lambda i, at: (0, 0)),
            ],
            out_specs=pl.BlockSpec((some, width), lambda i, at: (i, 0)),
        ),
        out_shape=jax.ShapeDtypeStruct((rows // YH, width), jnp.bfloat16),
    )(at, patches, gain[None])


def join_kernel(at_ref, p_ref, a0, a1, a2, a3, gain_ref, top_ref, low_ref, s_ref):
    mixed = a0[...].astype(jnp.float32)
    for ref in (a1, a2, a3):
        mixed += ref[...].astype(jnp.float32)
    mixed = p_ref[...].astype(jnp.float32) + mixed
    tiles, rows, lanes = s_ref.shape
    for t in range(tiles):
        s_ref[t] = mixed[:, t * lanes : (t + 1) * lanes]
    width, count, some = tiles * lanes, rows // 4, top_ref.shape[0]
    parts = [
        jnp.concatenate([s_ref[t, pl.ds(p, count, stride=4), :] for t in range(tiles)], axis=1)
        for p in range(4)
    ]
    mean = sum(jnp.sum(part, axis=-1, keepdims=True) for part in parts) / (4 * width)
    parts = [part - mean for part in parts]
    square = sum(jnp.sum(part * part, axis=-1, keepdims=True) for part in parts) / (4 * width)
    scale = lax.rsqrt(square + ln_epsilon)
    for p, part in enumerate(parts):
        here = slice(p * width, (p + 1) * width)
        out = (part * scale * gain_ref[:, here]).astype(top_ref.dtype)
        top_ref[:, here] = out[:some]
        low_ref[:, here] = out[some:]


def join_block(at, patches, parts, gain):
    rows, width = parts[0].shape
    shape = (rows // 8, 4 * width)

    def whole(*size):
        return pl.BlockSpec(size, lambda i, at: (0, 0))

    return pl.pallas_call(
        join_kernel,
        grid_spec=pltpu.PrefetchScalarGridSpec(
            num_scalar_prefetch=1,
            grid=(1,),
            in_specs=[pl.BlockSpec((rows, width), lambda i, at: (at[4] * X + at[3], 0))]
            + [whole(rows, width)] * 4
            + [whole(1, 4 * width)],
            out_specs=[whole(*shape)] * 2,
            scratch_shapes=[pltpu.VMEM((width // 128, rows, 128), jnp.float32)],
        ),
        out_shape=[jax.ShapeDtypeStruct(shape, jnp.bfloat16)] * 2,
    )(at, patches, *parts, gain[None])


def text_kernel(*refs):
    parts, (gain_ref, keep_ref, o_ref) = refs[:-3], refs[-3:]
    for n, ref in enumerate(parts):
        part = ref[...].astype(jnp.float32)
        square = jnp.mean(part * part, axis=-1, keepdims=True)
        part = part * lax.rsqrt(square + rms_epsilon) * gain_ref[...]
        o_ref[n] = (part * keep_ref[n]).astype(o_ref.dtype)


def text_block(pairs, gain, keep):
    rows, depth = pairs[0].shape[0] // 2, pairs[0].shape[1]
    steps, n = 4, 2 * len(pairs)
    some = rows // steps
    out = pl.pallas_call(
        text_kernel,
        grid=(steps,),
        in_specs=[pl.BlockSpec((some, depth), lambda i: (i, 0))] * len(pairs)
        + [pl.BlockSpec((some, depth), lambda i: (i + steps, 0))] * len(pairs)
        + [
            pl.BlockSpec((1, depth), lambda i: (0, 0)),
            pl.BlockSpec((n, some, 1), lambda i: (0, i, 0)),
        ],
        out_specs=pl.BlockSpec((n, some, depth), lambda i: (0, i, 0)),
        out_shape=jax.ShapeDtypeStruct((n, rows, depth), jnp.bfloat16),
    )(*pairs, *pairs, gain[None], keep.reshape(n, rows, 1))
    return out.reshape(n * rows, depth)


def shards(
    patches,
    counts,
    starts,
    embeds,
    route_ids,
    route_weights,
    vit_gain,
    vit_fc1,
    vit_fc2,
    proj_gain,
    proj_weight,
    moe_gain,
    shared_gate,
    shared_up,
    shared_down,
    expert_gate,
    expert_up,
    expert_down,
):
    xi, yi = lax.axis_index("x"), lax.axis_index("yh")
    rows = patches.shape[1]
    tok_dev = embeds.shape[1]
    seq_len = tok_dev * X * YH
    vtok = rows // 4
    capacity = seq_len // 8

    def padded(w):
        return jnp.pad(w, ((0, 0), (0, -w.shape[1] % 128)))

    vit_own = jnp.concatenate([padded(vit_fc1), padded(vit_fc2)], axis=1)
    wide = vit_own.shape[1] // 2
    vit = lax.all_gather(vit_own, ("yh",) + FSDP, axis=0, tiled=True).reshape(YH, -1, 2 * wide)
    experts = jnp.concatenate([expert_gate[:, 0], expert_up[:, 0], expert_down[:, 0]], axis=1)
    partner = lax.ppermute(experts, "yl", [(0, 1), (1, 0)])
    moe = lax.all_gather(
        jnp.concatenate([experts, partner], axis=1), ("z", "c"), axis=0, tiled=True
    )
    hid = expert_gate.shape[2]

    own = embeds[0]
    pair = jnp.concatenate([own, shift(own, 0, 1)], axis=0)
    stream = [pair] + [shift(pair, k, 0) for k in range(1, X)]
    proj = jnp.stack(ring(proj_weight, "z"))
    shared_own = [padded(shared_gate), padded(shared_up), padded(shared_down)]
    shared_own = jnp.concatenate(shared_own, axis=1)
    shared = jnp.stack(ring(shared_own, "z"))
    place_at = jnp.stack(
        [lax.axis_index("z"), yi * YH + lax.axis_index("yl"), lax.axis_index("c"), xi, yi]
    ).astype(jnp.int32)

    normed = norm_block(place_at, patches[0], vit_gain)
    vit, normed, proj, shared = tie(vit, normed, proj, shared)
    ahead = vit_block(jnp.stack([(xi + 2) % X, (xi + 1) % X]).astype(jnp.int32), normed, vit)
    got = [shift(ahead[0], 2, 0), shift(ahead[1], 1, 0)]
    rest = vit_block(jnp.stack([(xi + 3) % X, xi]).astype(jnp.int32), normed, vit)
    got += [shift(rest[0], 3, 0)]
    rest, proj, shared = tie(rest, proj, shared)
    proj = ring(proj, ("yh", "yl"))
    shared = [shared] + hops(shared, ("yh", "yl"), (1, 3))
    top, bottom = join_block(place_at, patches[0], [rest[1]] + got, proj_gain)
    left_top, right_bottom = shift(top, 1, 0), shift(bottom, -1, 0)
    left_bottom, right_top = shift(bottom, 1, 0), shift(top, -1, 0)
    far_top, far_bottom = shift(left_top, 1, 0), shift(right_bottom, -1, 0)
    left_bottom, right_top, proj = tie(left_bottom, right_top, proj)
    parts = [top, bottom, left_top, left_bottom, right_top, right_bottom, far_top, far_bottom]
    proj = proj + swap_cores(proj)
    visual = proj_block(place_at, parts, proj)
    visual, *shared = tie(visual, *shared)
    partner_visual = shift(visual, 0, 1)
    parts = [visual] + [shift(visual, k, 0) for k in range(1, X)]
    shared += hops(shared[0], ("yh", "yl"), (2,))
    parts += [partner_visual] + [shift(partner_visual, k, 0) for k in range(1, X)]
    swapped = swap_cores(shared[:3])
    whole, seen = seen_block(place_at, parts, moe_gain)
    whole, middle = tie(whole, shared[3])
    swapped += swap_cores([middle])
    own_core = [shared[0], shared[1], middle, shared[2]]
    shared = own_core + [swapped[0], swapped[1], swapped[3], swapped[2]]

    where = visual_positions(counts[0], starts[0], vtok)
    where = jnp.where(yi == 0, where, jnp.roll(where, vtok // YH))

    row = jnp.arange(seq_len, dtype=jnp.int32)
    row_x = (xi - row // tok_dev % X) % X
    row_y = (yi - row // (tok_dev * X)) % YH
    row_pos = (row_x * YH + row_y) * tok_dev + row % tok_dev
    take = row_pos[:, None] == where[None, :]
    is_visual = jnp.any(take, axis=1)
    rows_here = tok_dev * X

    text = text_block(stream, moe_gain, jnp.where(is_visual, 0.0, 1.0)[:, None])
    one_hot = take[:rows_here].astype(jnp.bfloat16)
    merged = jnp.where(
        is_visual[:tok_dev, None], dot(one_hot[:tok_dev], whole), own.astype(jnp.float32)
    )
    (merged,) = tie(merged)

    def ranks(expert):
        hit = route_ids[0] == expert
        chosen = jnp.any(hit, axis=1)
        share = jnp.sum(jnp.where(hit, route_weights[0], 0.0), axis=1)
        return jnp.where(chosen, jnp.cumsum(chosen.astype(jnp.int32)) - 1, -1), share

    slots = jnp.arange(capacity, dtype=jnp.int32)

    def routed(expert):
        rank, share = ranks(expert)
        place = rank[:, None] == slots[None, :]
        factor = jnp.sum(jnp.where(place, share[:, None], 0.0), axis=0)
        token_at = jnp.sum(jnp.where(place, row[:, None] + 1, 0), axis=0) - 1
        return token_at, factor

    token_at, factor = routed(xi * YH + yi)
    token_at_other, _ = routed(xi * YH + (yi + 1) % YH)
    pick_text = (token_at[:, None] == row_pos[None, :]).astype(jnp.bfloat16)
    pick_seen = (token_at[:, None] == where[None, :]).astype(jnp.bfloat16)
    low = lax.axis_index("yl").astype(jnp.int32)[None]
    values = expert_block(low, pick_text, pick_seen, text, seen, factor[:, None], moe, hid)
    values_other = shift(values, 0, 1)
    hidden = hidden_block(place_at, one_hot, seen, text, shared)
    args = (place_at, hidden, jnp.stack([token_at, token_at_other]), values, values_other, shared)
    far_sum, next_sum = down_block((2, 1), *args)
    sums = [shift(far_sum, -2, 0), shift(next_sum, -1, 0)]
    back_sum, own_sum = down_block((3, 0), *args)
    sums += [shift(back_sum, -3, 0)]
    total = merged + own_sum.astype(jnp.float32)
    for part in sums:
        total = total + part.astype(jnp.float32)
    return total.astype(jnp.bfloat16)[None]


def solution(mesh):
    fine = Mesh(mesh.devices.reshape(X, YH, 2, 4, 2), SEQ + FSDP)
    placed = (
        P(FSDP, None, None),
        P(FSDP, None),
        P(FSDP, None),
        P(FSDP, SEQ, None),
        P(FSDP, None, None),
        P(FSDP, None, None),
        P(),
        P(FSDP, SEQ),
        P(FSDP, SEQ),
        P(),
        P(FSDP, SEQ),
        P(),
        P(FSDP, SEQ),
        P(FSDP, SEQ),
        P(FSDP, SEQ),
        P(FSDP, SEQ, None),
        P(FSDP, SEQ, None),
        P(FSDP, SEQ, None),
    )

    return jax.shard_map(
        shards, mesh=fine, in_specs=placed, out_specs=P(FSDP, SEQ, None), check_vma=False
    )
```
